32 devices in a mesh: short: 8 (over z, y), long: 4 (over x, core).
Axes of the slice: x: 2, y: 2, z: 4, core: 2. Of those that a mesh axis runs over, the one named last changes fastest.
Arguments:
- query: bfloat16 [32768, 8, 128], P(('long', 'short')), may hold values from -6 to 6
- key: bfloat16 [32768, 8, 128], P(('long', 'short')), may hold values from -6 to 6
- value: bfloat16 [32768, 8, 128], P(('long', 'short')), may hold values from -6 to 6
- level_weight: float32 [8, 20, 32768], P(None, None, ('long', 'short')), may hold values from 0.25 to 1.75
Outputs:
- attended: bfloat16 [32768, 8, 128], P(('long', 'short'))
The draws below stay inside these ranges and needn't reach their ends.
All inputs are finite; a program needn't handle non-finite values.
Results may differ from the reference program's by a relative error of at most 0.0019.
Values sent between devices are 32-bit elements; how exact they have to be, the bound alone decides.
A program may use at most 128 MiB of HBM per device.

```python
import jax
import jax.numpy as jnp
from jax import lax

H = 8
DH = 128
TOK_DEV = 1024
LEVELS = 20
TOKENS = 32768
N_SHORT = 8
N_LONG = 4


def block_scale(stream_key, extent, cuts, smallest, largest):
    def one(axis_at, parts):
        draws = jax.random.uniform(jax.random.fold_in(jax.random.fold_in(stream_key, 6), axis_at), (parts,), jnp.float32, smallest / len(cuts), largest / len(cuts))
        return jnp.repeat(jnp.exp(draws), extent[axis_at] // parts).reshape((-1,) + (1,) * (len(extent) - axis_at - 1))

    level = one(*cuts[0])
    for cut in cuts[1:]:
        level = level * one(*cut)
    return level


def centred(stream_key, dims, deviation, limit, pieces=(), held_as=jnp.bfloat16):
    result = jax.random.normal(stream_key, dims, jnp.float32) * deviation
    if len(pieces) > 0:
        result = block_scale(stream_key, dims, pieces, -0.22, 0.18) * result
    return jnp.clip(result, min=-limit, max=limit).astype(held_as)


def setup_inputs(seed: int = 0) -> dict:
    streams_of = jax.random.split(jax.random.key(seed), 5)
    return {
        "query": centred(streams_of[0], (TOKENS, H, DH), 1.0, 6.0, ((0, 32),)),
        "key": centred(streams_of[1], (TOKENS, H, DH), 1.0, 6.0, ((0, 32),)),
        "value": centred(streams_of[2], (TOKENS, H, DH), 1.0, 6.0, ((0, 32),)),
        "level_weight": jnp.clip(0.25 + 1.5 * jax.random.uniform(streams_of[3], (H, LEVELS, TOKENS), jnp.float32) ** block_scale(streams_of[3], (H, LEVELS, TOKENS), ((2, 32),), -0.2, 0.2), 0.25, 1.75),
    }


EPSILON = 1e-06

def level_table(row_ids, col_ids, local_bits):
    differ = jnp.bitwise_xor(row_ids[:, None], col_ids[None, :])
    levels = jnp.zeros(differ.shape, jnp.int32)
    for bit_no in range(local_bits):
        levels = levels + (differ >= 1 << bit_no).astype(jnp.int32)
    return levels

def near_part(query_blk, key_blk, value_blk, weight_blk):
    length = query_blk.shape[0]
    local_bits = length.bit_length() - 1
    block_rows = min(512, length)
    col_ids = jnp.arange(length, dtype=jnp.int32)
    key_full = key_blk.astype(jnp.float32)
    value_full = value_blk.astype(jnp.float32)
    outputs = []
    for row_start in range(0, length, block_rows):
        row_ids = row_start + jnp.arange(block_rows, dtype=jnp.int32)
        levels = level_table(row_ids, col_ids, local_bits)
        causal = col_ids[None, :] <= row_ids[:, None]
        scores = jnp.einsum('thd,shd->hts', query_blk[row_start:row_start + block_rows].astype(jnp.float32), key_full)
        mixing = jnp.zeros(scores.shape, jnp.float32)
        for level_no in range(local_bits + 1):
            chosen = jnp.where(levels == level_no, 1.0, 0.0).astype(jnp.float32)
            mixing = mixing + chosen[None] * weight_blk[:, level_no, row_start:row_start + block_rows][:, :, None]
        weighted = jnp.where(causal[None], mixing * scores, 0.0).astype(jnp.bfloat16)
        outputs.append(jnp.einsum('hts,she->the', weighted.astype(jnp.float32), value_full))
    return jnp.concatenate(outputs, 0)

def far_part(query_blk, bucket_blk, weight_blk, local_bits):
    bit_count = bucket_blk.shape[0]
    products = jnp.einsum('thd,bhde->bthe', query_blk.astype(jnp.float32), bucket_blk, precision=lax.Precision.HIGHEST)
    gains = jnp.transpose(weight_blk[:, local_bits + 1:local_bits + 1 + bit_count, :], (1, 2, 0))
    return lax.optimization_barrier(jnp.sum(products * gains[..., None], 0))

def finish(total):
    scale = lax.rsqrt(lax.optimization_barrier(jnp.mean(total * total, -1, keepdims=True)) + EPSILON)
    return (total * scale).astype(jnp.bfloat16)

def state_of(inputs):
    return jnp.einsum('thd,the->hde', inputs[0].astype(jnp.float32), inputs[1].astype(jnp.float32))

def reference(query, key, value, level_weight):
    blocks = N_SHORT * N_LONG
    block_bits = blocks.bit_length() - 1
    local_bits = TOK_DEV.bit_length() - 1
    heads = query.shape[1]
    width = query.shape[2]
    query_b = query.reshape(blocks, TOK_DEV, heads, width)
    key_b = key.reshape(blocks, TOK_DEV, heads, width)
    value_b = value.reshape(blocks, TOK_DEV, heads, width)
    weight_b = jnp.transpose(level_weight.reshape(heads, LEVELS, blocks, TOK_DEV), (2, 0, 1, 3))
    states = lax.map(state_of, (key_b, value_b))
    block_ids = jnp.arange(blocks, dtype=jnp.int32)
    level_sum = states
    buckets = []
    for bit_no in range(block_bits):
        partner = jnp.bitwise_xor(block_ids >> bit_no, 1).astype(jnp.int32)
        chosen = jnp.take(level_sum, partner, axis=0)
        is_set = block_ids >> bit_no & 1 == 1
        buckets.append(jnp.where(is_set[:, None, None, None], chosen, 0.0))
        level_sum = level_sum.reshape((-1, 2) + level_sum.shape[1:]).sum(1)
    bucket_all = jnp.stack(buckets, 1)

    def one_block(items):
        query_blk, key_blk, value_blk, weight_blk, bucket_blk = items
        total = near_part(query_blk, key_blk, value_blk, weight_blk) + far_part(query_blk, bucket_blk, weight_blk, local_bits)
        return finish(total)
    attended = lax.map(one_block, (query_b, key_b, value_b, weight_b, bucket_all))
    return attended.reshape(blocks * TOK_DEV, heads, width)
```

```python
import functools

import jax
import jax.numpy as jnp
from jax import lax
from jax.experimental import pallas as pl
from jax.experimental.pallas import tpu as pltpu
from jax.sharding import PartitionSpec as P

EPSILON = 1e-06
TILE = 256
SUB = 128
STATE_TIME = 0.43
NEAR_TIME = 1.15
STEP = 1.31
LATENCY = 2.4
CORE_LATENCY = 1.0
MESH_ID = pl.DeviceIdType.MESH


def log2(n):
    return n.bit_length() - 1


def subsets(bits):
    found = [tuple(b for i, b in enumerate(bits) if mask >> i & 1) for mask in range(1 << len(bits))]
    return sorted(found, key=len)


def nt_dot(a, b):
    return lax.dot_general(a, b, (((1,), (1,)), ((), ())), preferred_element_type=jnp.float32)


def kernel(
    short_bits, long_bits, heads, length, width,
    q_ref, k_ref, v_ref, w_ref, out_ref,
    k_in, v_in, q_in, w_in, wide_a, wide_b, q_heads, k_heads, v_turned, near, levels, sums, buckets, send_sem, recv_sem, load_sem,
):
    bits = short_bits + long_bits
    rows = heads * width
    local_bits = log2(length)
    short_pos = lax.axis_index("short")
    long_pos = lax.axis_index("long")
    bit = [(short_pos // (1 << b)) % 2 for b in range(short_bits)]
    bit += [(long_pos // (1 << b)) % 2 for b in range(long_bits)]

    core = short_bits
    half = heads // 2
    targets = subsets([0, core - 2])

    def gateway(b):
        return bit[b - 1] + bit[b] - 2 * bit[b - 1] * bit[b]

    def peer(flips):
        short = short_pos
        long = long_pos
        for b in flips:
            if b < short_bits:
                short = short + (1 - 2 * bit[b]) * (1 << b)
            else:
                long = long + (1 - 2 * bit[b]) * (1 << b - short_bits)
        return {"short": short, "long": long}

    def mine(i):
        return bit[0] * half + i

    def other(i):
        return (1 - bit[0]) * half + i

    def rows_of(p):
        return pl.ds(pl.multiple_of(p * width, width), width)

    def copy(src, dst, b, p, bank, sent, to):
        where = rows_of(p)
        base = (3 * b + bank) * heads
        return pltpu.make_async_remote_copy(
            src_ref=src.at[b, where], dst_ref=dst.at[b, where],
            send_sem=send_sem.at[base + sent], recv_sem=recv_sem.at[base + p],
            device_id=peer(to), device_id_type=MESH_ID,
        )

    def cross(b, p):
        return copy(sums, buckets, b, p, 0, p, (b,) if b < 2 or b >= core else (b - 1, b))

    def relay(b, p):
        return copy(buckets, buckets, b, p, 1, p, (b - 1,))

    def share(b, p):
        return copy(buckets, buckets, b, p, 2, p, (0,) if b < core else (core,))

    def far_copy(b, p, n, m):
        return copy(sums, buckets, b, p, 0, n * (half // 2) + m, (b,) + targets[n])

    peers = [(b,) for b in (0, 1)] + [(b,) for b in range(1, core - 1) if b > 1] + [(b - 1, b) for b in range(2, core)]
    peers += [(core,)] + [(b,) + c for b in range(core + 1, bits) for c in targets]

    barrier = pltpu.get_barrier_semaphore()
    for flips in peers:
        pl.semaphore_signal(barrier, inc=1, device_id=peer(flips), device_id_type=MESH_ID)

    loads = [
        pltpu.make_async_copy(src, dst, load_sem.at[n])
        for n, (src, dst) in enumerate([(k_ref, k_in), (v_ref, v_in), (q_ref, q_in)])
    ]
    for h in range(heads):
        loads.append(pltpu.make_async_copy(w_ref.at[:, h, :], w_in.at[h], load_sem.at[3 + h]))
    for load in loads[:2]:
        load.start()

    part = 64

    def widen(src, dst):
        def step(i, _):
            at = pl.multiple_of(i * part, part)
            x = src[pl.ds(at, part)].astype(jnp.float32)
            dst[pl.ds(pl.multiple_of(at * heads, part * heads), part * heads), :] = x.reshape(part * heads, width)
            return 0
        lax.fori_loop(0, length // part, step, 0)

    loads[0].wait()
    widen(k_in, wide_a)
    loads[1].wait()
    for load in loads[2:]:
        load.start()
    widen(v_in, wide_b)

    def state_step(i, _):
        h = (1 - bit[0] + i // half * (2 * bit[0] - 1)) * half + i % half
        key = wide_a[pl.ds(h, length, stride=heads), :].astype(jnp.bfloat16)
        turned = wide_b[pl.ds(h, length, stride=heads), :].T.astype(jnp.bfloat16)
        k_heads[h] = key
        v_turned[h] = turned
        sums[0, pl.ds(pl.multiple_of(h * width, width), width), :] = jnp.dot(turned, key, preferred_element_type=jnp.float32)

        @pl.when(i == 0)
        def _():
            pl.semaphore_wait(barrier, len(peers))

        cross(0, h).start()
        return 0

    lax.fori_loop(0, heads, state_step, 0)

    row = lax.broadcasted_iota(jnp.int32, (SUB, SUB), 0)
    col = lax.broadcasted_iota(jnp.int32, (SUB, SUB), 1)
    differ = jnp.bitwise_xor(row, col)
    table = jnp.zeros((SUB, SUB), jnp.int32)
    for b in range(log2(SUB)):
        table = table + (differ >= 1 << b).astype(jnp.int32)
    levels[...] = jnp.where(row <= col, table, -1)

    loads[2].wait()
    widen(q_in, wide_a)
    for load in loads[3:]:
        load.wait()

    def near_head(h):
        q_heads[h] = wide_a[pl.ds(h, length, stride=heads), :].astype(jnp.bfloat16)
        level = levels[...]
        for ti in range(length // TILE):
            cols = pl.ds(ti * TILE, TILE)
            query = q_heads[h, cols, :]
            total = None
            for si in range(ti + 1):
                scores = nt_dot(k_heads[h, pl.ds(si * TILE, TILE), :], query)
                if si < ti:
                    weighted = scores * w_in[h, pl.ds(log2(TILE) + (ti ^ si).bit_length(), 1), cols]
                else:
                    columns = []
                    for a in range(TILE // SUB):
                        at = pl.ds(ti * TILE + a * SUB, SUB)
                        parts = []
                        for c in range(TILE // SUB):
                            block = scores[c * SUB : (c + 1) * SUB, a * SUB : (a + 1) * SUB]
                            if c < a:
                                parts.append(block * w_in[h, pl.ds(log2(SUB) + (a ^ c).bit_length(), 1), at])
                            elif c > a:
                                parts.append(jnp.zeros_like(block))
                            else:
                                mixing = jnp.zeros((SUB, SUB), jnp.float32)
                                for n in range(log2(SUB) + 1):
                                    mixing = jnp.where(level == n, w_in[h, pl.ds(n, 1), at], mixing)
                                parts.append(mixing * block)
                        columns.append(jnp.concatenate(parts, 0))
                    weighted = jnp.concatenate(columns, 1)
                product = jnp.dot(
                    v_turned[h, :, pl.ds(si * TILE, TILE)], weighted.astype(jnp.bfloat16),
                    preferred_element_type=jnp.float32,
                )
                total = product if total is None else total + product
            near[h, :, cols] = total

    def add_up(b, p):
        if b < bits - 1:
            where = rows_of(p)
            sums[b + 1, where, :] = sums[b, where, :] + buckets[b, where, :]

    def when_low(b, do):
        if b < bits - 1 and b != core:
            do()
        else:
            pl.when(bit[b] == 0)(do)

    def when_high(b, do):
        if b < bits - 1 and b != core:
            do()
        else:
            pl.when(bit[b] == 1)(do)

    def when_gateway(b, do, yes=1):
        pl.when(gateway(b) == yes)(do)

    def by_core(m, away=False):
        return 2 * m + (1 - bit[core] if away else bit[core])

    events = []
    free = {}

    def flight(link, ready, step, latency):
        end = max(free.get(link, 0), ready) + step
        free[link] = end
        return end + latency

    def event(at, do, *given):
        events.append((at, functools.partial(do, *given)))

    def begin(b, side, i):
        p = side(i)
        if b < 2:
            cross(b, p).start()
        elif b < core:
            if side is mine:
                when_gateway(b, lambda: cross(b, p).start())
        elif b == core:
            if side is mine and bits > core + 1:
                @pl.when(gateway(core - 1) + 1 - bit[core] > 0)
                def _():
                    cross(b, p).start()
            else:
                when_low(b, lambda: cross(b, p).start())

    def arrived(b, side, i):
        p = side(i)
        cross(b, p).wait_recv()
        add_up(b, p)
        begin(b + 1, side, i)

    def cross_arrived(b, i):
        def do():
            p = mine(i)
            cross(b, p).wait_recv()
            relay(b, p).start()
            share(b, p).start()
            add_up(b, p)
            begin(b + 1, mine, i)
        when_gateway(b, do)

    def relay_arrived(b, i):
        def do():
            p = mine(i)
            relay(b, p).wait_recv()
            share(b, p).start()
            add_up(b, p)
            begin(b + 1, mine, i)
        when_gateway(b, do, 0)

    def share_arrived(b, yes, i):
        def do():
            p = other(i)
            share(b, p).wait_recv()
            add_up(b, p)
            begin(b + 1, other, i)
        when_gateway(b, do, yes)

    def core_pair(m):
        def do():
            for i in (2 * m, 2 * m + 1):
                cross(core, mine(i)).wait_recv()
            add_up(core, mine(by_core(m)))
            begin_far(core + 1, m)
        if bits > core + 1:
            when_gateway(core - 1, do)

    def core_arrived(side, yes, i):
        def do():
            when_high(core, lambda: cross(core, side(i)).wait_recv())
        when_gateway(core - 1, do, yes)

    def begin_far(b, m):
        def do():
            for n in range(len(targets)):
                far_copy(b, mine(by_core(m)), n, m).start()
        if b < bits:
            when_low(b, do)

    def far_arrived(b, side, m):
        p = side(by_core(m))

        def do():
            far_copy(b, p, 0, 0).wait_recv()
            share(b, p).start()
        when_high(b, do)
        if side is mine and b < bits - 1:
            def on():
                add_up(b, p)
                begin_far(b + 1, m)
            when_gateway(core - 1, on)

    def far_share_arrived(b, side, m):
        when_high(b, lambda: share(b, side(by_core(m, True))).wait_recv())

    when = {}
    for n, (side, i) in enumerate([(mine, i) for i in range(half)] + [(other, i) for i in range(half)]):
        when[side, i] = flight(0, STATE_TIME * (n + 1), STEP, LATENCY)
    for b in range(2):
        later = {}
        for (side, i), at in sorted(when.items(), key=lambda e: e[1]):
            event(at, arrived, b, side, i)
            later[side, i] = flight(1, at, STEP, LATENCY)
        if b == 0:
            when = later
    whole_at = dict(when)
    early = {}
    for b in range(2, core):
        later = {}
        for i in range(half):
            at = flight(("gate", b), when[mine, i], STEP, LATENCY)
            event(at, cross_arrived, b, i)
            early[i] = at
            near_share = max(flight(("share", b), at, STEP, LATENCY), when[other, i] + 0.01)
            event(near_share, share_arrived, b, 1, i)
            relayed = max(flight(("relay", b), at, STEP, LATENCY), when[mine, i] + 0.01)
            event(relayed, relay_arrived, b, i)
            last = max(flight(("last", b), relayed, STEP, LATENCY), when[other, i] + 0.01)
            event(last, share_arrived, b, 0, i)
            later[mine, i] = relayed
            later[other, i] = last
            if b == core - 1:
                if bits == core + 1:
                    event(at + CORE_LATENCY, core_arrived, mine, 1, i)
                event(near_share + CORE_LATENCY, core_arrived, other, 1, i)
                event(relayed + CORE_LATENCY, core_arrived, mine, 0, i)
                event(last + CORE_LATENCY, core_arrived, other, 0, i)
        when = later
    done = {i: max(when[mine, i], when[other, i]) + CORE_LATENCY for i in range(half)}
    for m in range(half // 2):
        at = early[2 * m + 1] + CORE_LATENCY
        event(at, core_pair, m)
        for b in range(core + 1, bits):
            for side in (mine, other):
                landed = flight(b, at, STEP, LATENCY + 0.7)
                event(landed, far_arrived, b, side, m)
                event(landed + CORE_LATENCY, far_share_arrived, b, side, m)
            at = landed
            for i in (2 * m, 2 * m + 1):
                done[i] = max(done[i], landed + CORE_LATENCY)

    def far_head(h, chosen, last):
        where = pl.ds(pl.multiple_of(h * width, width), width)
        high = []
        low = []
        for b in chosen:
            whole = jnp.where(bit[b] == 1, buckets[b, where, :], 0.0)
            top = whole.astype(jnp.bfloat16)
            high.append(top)
            low.append((whole - top.astype(jnp.float32)).astype(jnp.bfloat16))
        both = jnp.concatenate([jnp.concatenate(high, 0), jnp.concatenate(low, 0)], 1)
        for ti in range(length // TILE):
            cols = pl.ds(ti * TILE, TILE)
            query = q_heads[h, cols, :]
            products = nt_dot(both, jnp.concatenate([query, query], 1))
            total = near[h, :, cols]
            for n, b in enumerate(chosen):
                total = total + products[n * width : (n + 1) * width] * w_in[h, pl.ds(local_bits + 1 + b, 1), cols]
            if last:
                scale = lax.rsqrt(jnp.mean(total * total, 0, keepdims=True) + EPSILON)
                wide_b[pl.ds(ti * TILE * heads + h, TILE, stride=heads), :] = (total * scale).T
            else:
                near[h, :, cols] = total

    first = [0, 1]
    last = list(range(2, bits))
    loops = [
        (heads, NEAR_TIME, [0] * heads, lambda i: near_head(i)),
        (half, 0.43, [whole_at[mine, i] for i in range(half)], lambda i: far_head(mine(i), first, False)),
        (half, 0.43, [whole_at[other, i] for i in range(half)], lambda i: far_head(other(i), first, False)),
        (half, 1.2, [done[i] for i in range(half)], lambda i: (far_head(mine(i), last, True), far_head(other(i), last, True))),
    ]
    waiting = sorted(events, key=lambda e: e[0])
    clock = STATE_TIME * heads
    for count, cost, needs, work in loops:
        slots = []
        for need in needs:
            slots.append([])
            while waiting and waiting[0][0] <= max(clock, need + 0.02):
                at, do = waiting.pop(0)
                slots[-1].append(do)
                clock = max(clock, at)
            clock += cost

        def one(i, _, slots=slots, work=work):
            for at, group in enumerate(slots):
                def run(group=group):
                    for do in group:
                        do()
                if group:
                    pl.when(i == at)(run)
            work(i)
            return 0

        lax.fori_loop(0, count, one, 0)
    assert not waiting

    def narrow(i, _):
        at = pl.multiple_of(i * part, part)
        x = wide_b[pl.ds(pl.multiple_of(at * heads, part * heads), part * heads), :]
        out_ref[pl.ds(at, part)] = x.reshape(part, heads, width).astype(jnp.bfloat16)
        return 0

    lax.fori_loop(0, length // part, narrow, 0)

    def sent(i, _):
        for side in (mine, other):
            p = side(i)
            for b in range(2):
                cross(b, p).wait_send()
            if side is mine and bits > core + 1:
                @pl.when(gateway(core - 1) + 1 - bit[core] > 0)
                def _():
                    cross(core, p).wait_send()
            else:
                when_low(core, lambda: cross(core, p).wait_send())
        for b in range(2, core):
            share(b, mine(i)).wait_send()

            def do():
                cross(b, mine(i)).wait_send()
                relay(b, mine(i)).wait_send()
            when_gateway(b, do)
        return 0

    lax.fori_loop(0, half, sent, 0)

    def far_sent(m, _):
        for b in range(core + 1, bits):
            def do():
                for n in range(len(targets)):
                    far_copy(b, mine(by_core(m)), n, m).wait_send()
            when_gateway(core - 1, lambda: when_low(b, do))

            def do_share():
                for side in (mine, other):
                    share(b, side(by_core(m))).wait_send()
            when_high(b, do_share)
        return 0

    lax.fori_loop(0, half // 2, far_sent, 0)


def per_device(query, key, value, level_weight):
    length, heads, width = query.shape
    short_bits = log2(lax.axis_size("short"))
    long_bits = log2(lax.axis_size("long"))
    bits = short_bits + long_bits
    rows = heads * width
    copies = 3 * bits * heads
    level_weight = jnp.transpose(level_weight, (1, 0, 2))
    return pl.pallas_call(
        functools.partial(kernel, short_bits, long_bits, heads, length, width),
        out_shape=jax.ShapeDtypeStruct(query.shape, jnp.bfloat16),
        in_specs=[pl.BlockSpec(memory_space=pl.ANY)] * 4,
        out_specs=pl.BlockSpec(memory_space=pltpu.VMEM),
        scratch_shapes=[
            pltpu.VMEM(query.shape, jnp.bfloat16),
            pltpu.VMEM(query.shape, jnp.bfloat16),
            pltpu.VMEM(query.shape, jnp.bfloat16),
            pltpu.VMEM((heads, level_weight.shape[0], length), jnp.float32),
            pltpu.VMEM((length * heads, width), jnp.float32),
            pltpu.VMEM((length * heads, width), jnp.float32),
            pltpu.VMEM((heads, length, width), jnp.bfloat16),
            pltpu.VMEM((heads, length, width), jnp.bfloat16),
            pltpu.VMEM((heads, width, length), jnp.bfloat16),
            pltpu.VMEM((heads, width, length), jnp.float32),
            pltpu.VMEM((SUB, SUB), jnp.int32),
            pltpu.VMEM((bits, rows, width), jnp.float32),
            pltpu.VMEM((bits, rows, width), jnp.float32),
            pltpu.SemaphoreType.DMA((copies,)),
            pltpu.SemaphoreType.DMA((copies,)),
            pltpu.SemaphoreType.DMA((3 + heads,)),
        ],
        compiler_params=pltpu.CompilerParams(
            collective_id=0, has_side_effects=True, vmem_limit_bytes=60 * 1024 * 1024
        ),
    )(query, key, value, level_weight)


def solution(mesh):
    rows = P(("long", "short"), None)
    return jax.shard_map(
        per_device,
        mesh=mesh,
        in_specs=(rows, rows, rows, P(None, None, ("long", "short"))),
        out_specs=rows,
        check_vma=False,
    )
```

```python
import functools

import jax
import jax.numpy as jnp
from jax import lax
from jax.experimental import pallas as pl
from jax.experimental.pallas import tpu as pltpu
from jax.sharding import PartitionSpec as P

EPSILON = 1e-06
TILE = 256
SUB = 128
STATE_TIME = 0.43
NEAR_TIME = 1.15
STEP = 1.31
LATENCY = 2.4
CORE_LATENCY = 1.0
MESH_ID = pl.DeviceIdType.MESH


def log2(n):
    return n.bit_length() - 1


def subsets(bits):
    found = [tuple(b for i, b in enumerate(bits) if mask >> i & 1) for mask in range(1 << len(bits))]
    return sorted(found, key=len)


def nt_dot(a, b):
    return lax.dot_general(a, b, (((1,), (1,)), ((), ())), preferred_element_type=jnp.float32)


def kernel(
    short_bits, long_bits, heads, length, width,
    q_ref, k_ref, v_ref, w_ref, wide_b,
    k_in, v_in, q_in, w_in, wide_a, q_heads, k_heads, v_turned, near, levels, sums, buckets, send_sem, recv_sem, load_sem,
):
    bits = short_bits + long_bits
    rows = heads * width
    local_bits = log2(length)
    short_pos = lax.axis_index("short")
    long_pos = lax.axis_index("long")
    bit = [(short_pos // (1 << b)) % 2 for b in range(short_bits)]
    bit += [(long_pos // (1 << b)) % 2 for b in range(long_bits)]

    core = short_bits
    half = heads // 2
    targets = subsets([0, core - 2])

    def gateway(b):
        return bit[b - 1] + bit[b] - 2 * bit[b - 1] * bit[b]

    def peer(flips):
        short = short_pos
        long = long_pos
        for b in flips:
            if b < short_bits:
                short = short + (1 - 2 * bit[b]) * (1 << b)
            else:
                long = long + (1 - 2 * bit[b]) * (1 << b - short_bits)
        return {"short": short, "long": long}

    def mine(i):
        return bit[0] * half + i

    def other(i):
        return (1 - bit[0]) * half + i

    def rows_of(p):
        return pl.ds(pl.multiple_of(p * width, width), width)

    def copy(src, dst, b, p, bank, sent, to):
        where = rows_of(p)
        base = (3 * b + bank) * heads
        return pltpu.make_async_remote_copy(
            src_ref=src.at[b, where], dst_ref=dst.at[b, where],
            send_sem=send_sem.at[base + sent], recv_sem=recv_sem.at[base + p],
            device_id=peer(to), device_id_type=MESH_ID,
        )

    def cross(b, p):
        return copy(sums, buckets, b, p, 0, p, (b,) if b < 2 or b >= core else (b - 1, b))

    def relay(b, p):
        return copy(buckets, buckets, b, p, 1, p, (b - 1,))

    def share(b, p):
        return copy(buckets, buckets, b, p, 2, p, (0,) if b < core else (core,))

    def far_copy(b, p, n, m):
        return copy(sums, buckets, b, p, 0, n * (half // 2) + m, (b,) + targets[n])

    peers = [(b,) for b in (0, 1)] + [(b,) for b in range(1, core - 1) if b > 1] + [(b - 1, b) for b in range(2, core)]
    peers += [(core,)] + [(b,) + c for b in range(core + 1, bits) for c in targets]

    barrier = pltpu.get_barrier_semaphore()
    for flips in peers:
        pl.semaphore_signal(barrier, inc=1, device_id=peer(flips), device_id_type=MESH_ID)

    loads = [
        pltpu.make_async_copy(src, dst, load_sem.at[n])
        for n, (src, dst) in enumerate([(k_ref, k_in), (v_ref, v_in), (q_ref, q_in)])
    ]
    for h in range(heads):
        loads.append(pltpu.make_async_copy(w_ref.at[:, h, :], w_in.at[h], load_sem.at[3 + h]))
    for load in loads[:2]:
        load.start()

    part = 64

    def widen(src, dst):
        def step(i, _):
            at = pl.multiple_of(i * part, part)
            x = src[pl.ds(at, part)].astype(jnp.float32)
            dst[pl.ds(pl.multiple_of(at * heads, part * heads), part * heads), :] = x.reshape(part * heads, width)
            return 0
        lax.fori_loop(0, length // part, step, 0)

    loads[0].wait()
    widen(k_in, wide_a)
    loads[1].wait()
    for load in loads[2:]:
        load.start()
    widen(v_in, wide_b)

    def state_step(i, _):
        h = (1 - bit[0] + i // half * (2 * bit[0] - 1)) * half + i % half
        key = wide_a[pl.ds(h, length, stride=heads), :].astype(jnp.bfloat16)
        turned = wide_b[pl.ds(h, length, stride=heads), :].T.astype(jnp.bfloat16)
        k_heads[h] = key
        v_turned[h] = turned
        sums[0, pl.ds(pl.multiple_of(h * width, width), width), :] = jnp.dot(turned, key, preferred_element_type=jnp.float32)

        @pl.when(i == 0)
        def _():
            pl.semaphore_wait(barrier, len(peers))

        cross(0, h).start()
        return 0

    lax.fori_loop(0, heads, state_step, 0)

    row = lax.broadcasted_iota(jnp.int32, (SUB, SUB), 0)
    col = lax.broadcasted_iota(jnp.int32, (SUB, SUB), 1)
    differ = jnp.bitwise_xor(row, col)
    table = jnp.zeros((SUB, SUB), jnp.int32)
    for b in range(log2(SUB)):
        table = table + (differ >= 1 << b).astype(jnp.int32)
    levels[...] = jnp.where(row <= col, table, -1)

    loads[2].wait()
    widen(q_in, wide_a)
    for load in loads[3:]:
        load.wait()

    def near_head(h):
        q_heads[h] = wide_a[pl.ds(h, length, stride=heads), :].astype(jnp.bfloat16)
        level = levels[...]
        for ti in range(length // TILE):
            cols = pl.ds(ti * TILE, TILE)
            query = q_heads[h, cols, :]
            total = None
            for si in range(ti + 1):
                scores = nt_dot(k_heads[h, pl.ds(si * TILE, TILE), :], query)
                if si < ti:
                    weighted = scores * w_in[h, pl.ds(log2(TILE) + (ti ^ si).bit_length(), 1), cols]
                else:
                    columns = []
                    for a in range(TILE // SUB):
                        at = pl.ds(ti * TILE + a * SUB, SUB)
                        parts = []
                        for c in range(TILE // SUB):
                            block = scores[c * SUB : (c + 1) * SUB, a * SUB : (a + 1) * SUB]
                            if c < a:
                                parts.append(block * w_in[h, pl.ds(log2(SUB) + (a ^ c).bit_length(), 1), at])
                            elif c > a:
                                parts.append(jnp.zeros_like(block))
                            else:
                                mixing = jnp.zeros((SUB, SUB), jnp.float32)
                                for n in range(log2(SUB) + 1):
                                    mixing = jnp.where(level == n, w_in[h, pl.ds(n, 1), at], mixing)
                                parts.append(mixing * block)
                        columns.append(jnp.concatenate(parts, 0))
                    weighted = jnp.concatenate(columns, 1)
                product = jnp.dot(
                    v_turned[h, :, pl.ds(si * TILE, TILE)], weighted.astype(jnp.bfloat16),
                    preferred_element_type=jnp.float32,
                )
                total = product if total is None else total + product
            near[h, :, cols] = total

    def add_up(b, p):
        if b < bits - 1:
            where = rows_of(p)
            sums[b + 1, where, :] = sums[b, where, :] + buckets[b, where, :]

    def when_low(b, do):
        if b < bits - 1 and b != core:
            do()
        else:
            pl.when(bit[b] == 0)(do)

    def when_high(b, do):
        if b < bits - 1 and b != core:
            do()
        else:
            pl.when(bit[b] == 1)(do)

    def when_gateway(b, do, yes=1):
        pl.when(gateway(b) == yes)(do)

    def by_core(m, away=False):
        return 2 * m + (1 - bit[core] if away else bit[core])

    events = []
    free = {}

    def flight(link, ready, step, latency):
        end = max(free.get(link, 0), ready) + step
        free[link] = end
        return end + latency

    def event(at, do, *given):
        events.append((at, functools.partial(do, *given)))

    def begin(b, side, i):
        p = side(i)
        if b < 2:
            cross(b, p).start()
        elif b < core:
            if side is mine:
                when_gateway(b, lambda: cross(b, p).start())
        elif b == core:
            if side is mine and bits > core + 1:
                @pl.when(gateway(core - 1) + 1 - bit[core] > 0)
                def _():
                    cross(b, p).start()
            else:
                when_low(b, lambda: cross(b, p).start())

    def arrived(b, side, i):
        p = side(i)
        cross(b, p).wait_recv()
        add_up(b, p)
        begin(b + 1, side, i)

    def cross_arrived(b, i):
        def do():
            p = mine(i)
            cross(b, p).wait_recv()
            relay(b, p).start()
            share(b, p).start()
            add_up(b, p)
            begin(b + 1, mine, i)
        when_gateway(b, do)

    def relay_arrived(b, i):
        def do():
            p = mine(i)
            relay(b, p).wait_recv()
            share(b, p).start()
            add_up(b, p)
            begin(b + 1, mine, i)
        when_gateway(b, do, 0)

    def share_arrived(b, yes, i):
        def do():
            p = other(i)
            share(b, p).wait_recv()
            add_up(b, p)
            begin(b + 1, other, i)
        when_gateway(b, do, yes)

    def core_pair(m):
        def do():
            for i in (2 * m, 2 * m + 1):
                cross(core, mine(i)).wait_recv()
            add_up(core, mine(by_core(m)))
            begin_far(core + 1, m)
        if bits > core + 1:
            when_gateway(core - 1, do)

    def core_arrived(side, yes, i):
        def do():
            when_high(core, lambda: cross(core, side(i)).wait_recv())
        when_gateway(core - 1, do, yes)

    def begin_far(b, m):
        def do():
            for n in range(len(targets)):
                far_copy(b, mine(by_core(m)), n, m).start()
        if b < bits:
            when_low(b, do)

    def far_arrived(b, side, m):
        p = side(by_core(m))

        def do():
            far_copy(b, p, 0, 0).wait_recv()
            share(b, p).start()
        when_high(b, do)
        if side is mine and b < bits - 1:
            def on():
                add_up(b, p)
                begin_far(b + 1, m)
            when_gateway(core - 1, on)

    def far_share_arrived(b, side, m):
        when_high(b, lambda: share(b, side(by_core(m, True))).wait_recv())

    when = {}
    for n, (side, i) in enumerate([(mine, i) for i in range(half)] + [(other, i) for i in range(half)]):
        when[side, i] = flight(0, STATE_TIME * (n + 1), STEP, LATENCY)
    for b in range(2):
        later = {}
        for (side, i), at in sorted(when.items(), key=lambda e: e[1]):
            event(at, arrived, b, side, i)
            later[side, i] = flight(1, at, STEP, LATENCY)
        if b == 0:
            when = later
    whole_at = dict(when)
    early = {}
    for b in range(2, core):
        later = {}
        for i in range(half):
            at = flight(("gate", b), when[mine, i], STEP, LATENCY)
            event(at, cross_arrived, b, i)
            early[i] = at
            near_share = max(flight(("share", b), at, STEP, LATENCY), when[other, i] + 0.01)
            event(near_share, share_arrived, b, 1, i)
            relayed = max(flight(("relay", b), at, STEP, LATENCY), when[mine, i] + 0.01)
            event(relayed, relay_arrived, b, i)
            last = max(flight(("last", b), relayed, STEP, LATENCY), when[other, i] + 0.01)
            event(last, share_arrived, b, 0, i)
            later[mine, i] = relayed
            later[other, i] = last
            if b == core - 1:
                if bits == core + 1:
                    event(at + CORE_LATENCY, core_arrived, mine, 1, i)
                event(near_share + CORE_LATENCY, core_arrived, other, 1, i)
                event(relayed + CORE_LATENCY, core_arrived, mine, 0, i)
                event(last + CORE_LATENCY, core_arrived, other, 0, i)
        when = later
    done = {i: max(when[mine, i], when[other, i]) + CORE_LATENCY for i in range(half)}
    for m in range(half // 2):
        at = early[2 * m + 1] + CORE_LATENCY
        event(at, core_pair, m)
        for b in range(core + 1, bits):
            for side in (mine, other):
                landed = flight(b, at, STEP, LATENCY + 0.7)
                event(landed, far_arrived, b, side, m)
                event(landed + CORE_LATENCY, far_share_arrived, b, side, m)
            at = landed
            for i in (2 * m, 2 * m + 1):
                done[i] = max(done[i], landed + CORE_LATENCY)

    def far_head(h, chosen, last):
        where = pl.ds(pl.multiple_of(h * width, width), width)
        high = []
        low = []
        for b in chosen:
            whole = jnp.where(bit[b] == 1, buckets[b, where, :], 0.0)
            top = whole.astype(jnp.bfloat16)
            high.append(top)
            low.append((whole - top.astype(jnp.float32)).astype(jnp.bfloat16))
        both = jnp.concatenate([jnp.concatenate(high, 0), jnp.concatenate(low, 0)], 1)
        for ti in range(length // TILE):
            cols = pl.ds(ti * TILE, TILE)
            query = q_heads[h, cols, :]
            products = nt_dot(both, jnp.concatenate([query, query], 1))
            total = near[h, :, cols]
            for n, b in enumerate(chosen):
                total = total + products[n * width : (n + 1) * width] * w_in[h, pl.ds(local_bits + 1 + b, 1), cols]
            if last:
                scale = lax.rsqrt(jnp.mean(total * total, 0, keepdims=True) + EPSILON)
                wide_b[pl.ds(ti * TILE * heads + h, TILE, stride=heads), :] = (total * scale).T
            else:
                near[h, :, cols] = total

    first = [0, 1]
    last = list(range(2, bits))
    loops = [
        (heads, NEAR_TIME, [0] * heads, lambda i: near_head(i)),
        (half, 0.43, [whole_at[mine, i] for i in range(half)], lambda i: far_head(mine(i), first, False)),
        (half, 0.43, [whole_at[other, i] for i in range(half)], lambda i: far_head(other(i), first, False)),
        (half, 1.2, [done[i] for i in range(half)], lambda i: (far_head(mine(i), last, True), far_head(other(i), last, True))),
    ]
    waiting = sorted(events, key=lambda e: e[0])
    clock = STATE_TIME * heads
    for count, cost, needs, work in loops:
        slots = []
        for need in needs:
            slots.append([])
            while waiting and waiting[0][0] <= max(clock, need + 0.02):
                at, do = waiting.pop(0)
                slots[-1].append(do)
                clock = max(clock, at)
            clock += cost

        def one(i, _, slots=slots, work=work):
            for at, group in enumerate(slots):
                def run(group=group):
                    for do in group:
                        do()
                if group:
                    pl.when(i == at)(run)
            work(i)
            return 0

        lax.fori_loop(0, count, one, 0)
    assert not waiting

    def sent(i, _):
        for side in (mine, other):
            p = side(i)
            for b in range(2):
                cross(b, p).wait_send()
            if side is mine and bits > core + 1:
                @pl.when(gateway(core - 1) + 1 - bit[core] > 0)
                def _():
                    cross(core, p).wait_send()
            else:
                when_low(core, lambda: cross(core, p).wait_send())
        for b in range(2, core):
            share(b, mine(i)).wait_send()

            def do():
                cross(b, mine(i)).wait_send()
                relay(b, mine(i)).wait_send()
            when_gateway(b, do)
        return 0

    lax.fori_loop(0, half, sent, 0)

    def far_sent(m, _):
        for b in range(core + 1, bits):
            def do():
                for n in range(len(targets)):
                    far_copy(b, mine(by_core(m)), n, m).wait_send()
            when_gateway(core - 1, lambda: when_low(b, do))

            def do_share():
                for side in (mine, other):
                    share(b, side(by_core(m))).wait_send()
            when_high(b, do_share)
        return 0

    lax.fori_loop(0, half // 2, far_sent, 0)


def per_device(query, key, value, level_weight):
    length, heads, width = query.shape
    short_bits = log2(lax.axis_size("short"))
    long_bits = log2(lax.axis_size("long"))
    bits = short_bits + long_bits
    rows = heads * width
    copies = 3 * bits * heads
    level_weight = jnp.transpose(level_weight, (1, 0, 2))
    total = pl.pallas_call(
        functools.partial(kernel, short_bits, long_bits, heads, length, width),
        out_shape=pltpu.VMEM((length * heads, width), jnp.float32),
        in_specs=[pl.BlockSpec(memory_space=pl.ANY)] * 4,
        out_specs=pl.BlockSpec(memory_space=pltpu.VMEM),
        scratch_shapes=[
            pltpu.VMEM(query.shape, jnp.bfloat16),
            pltpu.VMEM(query.shape, jnp.bfloat16),
            pltpu.VMEM(query.shape, jnp.bfloat16),
            pltpu.VMEM((heads, level_weight.shape[0], length), jnp.float32),
            pltpu.VMEM((length * heads, width), jnp.float32),
            pltpu.VMEM((heads, length, width), jnp.bfloat16),
            pltpu.VMEM((heads, length, width), jnp.bfloat16),
            pltpu.VMEM((heads, width, length), jnp.bfloat16),
            pltpu.VMEM((heads, width, length), jnp.float32),
            pltpu.VMEM((SUB, SUB), jnp.int32),
            pltpu.VMEM((bits, rows, width), jnp.float32),
            pltpu.VMEM((bits, rows, width), jnp.float32),
            pltpu.SemaphoreType.DMA((copies,)),
            pltpu.SemaphoreType.DMA((copies,)),
            pltpu.SemaphoreType.DMA((3 + heads,)),
        ],
        compiler_params=pltpu.CompilerParams(
            collective_id=0, has_side_effects=True, vmem_limit_bytes=52 * 1024 * 1024
        ),
    )(query, key, value, level_weight)
    return total.reshape(query.shape).astype(jnp.bfloat16)


def solution(mesh):
    rows = P(("long", "short"), None)
    return jax.shard_map(
        per_device,
        mesh=mesh,
        in_specs=(rows, rows, rows, P(None, None, ("long", "short"))),
        out_specs=rows,
        check_vma=False,
    )
```

```python
import functools

import jax
import jax.numpy as jnp
from jax import lax
from jax.experimental import pallas as pl
from jax.experimental.pallas import tpu as pltpu
from jax.sharding import PartitionSpec as P

EPSILON = 1e-06
TILE = 256
SUB = 128
STATE_TIME = 0.43
NEAR_TIME = 1.15
STEP = 1.31
LATENCY = 2.4
CORE_LATENCY = 1.0
CHUNKS = 4
MESH_ID = pl.DeviceIdType.MESH


def log2(n):
    return n.bit_length() - 1


def subsets(bits):
    found = [tuple(b for i, b in enumerate(bits) if mask >> i & 1) for mask in range(1 << len(bits))]
    return sorted(found, key=len)


def nt_dot(a, b):
    return lax.dot_general(a, b, (((1,), (1,)), ((), ())), preferred_element_type=jnp.float32)


def kernel(
    short_bits, long_bits, heads, length, width,
    q_ref, k_ref, v_ref, w_ref, wide_b,
    k_in, v_in, q_in, w_in, wide_a, q_heads, k_heads, v_turned, near, levels, sums, buckets, send_sem, recv_sem, load_sem,
):
    bits = short_bits + long_bits
    rows = heads * width
    local_bits = log2(length)
    short_pos = lax.axis_index("short")
    long_pos = lax.axis_index("long")
    bit = [(short_pos // (1 << b)) % 2 for b in range(short_bits)]
    bit += [(long_pos // (1 << b)) % 2 for b in range(long_bits)]

    core = short_bits
    half = heads // 2
    targets = subsets([0, core - 2])

    def gateway(b):
        return bit[b - 1] + bit[b] - 2 * bit[b - 1] * bit[b]

    def peer(flips):
        short = short_pos
        long = long_pos
        for b in flips:
            if b < short_bits:
                short = short + (1 - 2 * bit[b]) * (1 << b)
            else:
                long = long + (1 - 2 * bit[b]) * (1 << b - short_bits)
        return {"short": short, "long": long}

    def mine(i):
        return bit[0] * half + i

    def other(i):
        return (1 - bit[0]) * half + i

    def rows_of(p):
        return pl.ds(pl.multiple_of(p * width, width), width)

    def copy(src, dst, b, p, bank, sent, to):
        where = rows_of(p)
        base = (3 * b + bank) * heads
        return pltpu.make_async_remote_copy(
            src_ref=src.at[b, where], dst_ref=dst.at[b, where],
            send_sem=send_sem.at[base + sent], recv_sem=recv_sem.at[base + p],
            device_id=peer(to), device_id_type=MESH_ID,
        )

    def cross(b, p):
        return copy(sums, buckets, b, p, 0, p, (b,) if b < 2 or b >= core else (b - 1, b))

    def relay(b, p):
        return copy(buckets, buckets, b, p, 1, p, (b - 1,))

    def share(b, p):
        return copy(buckets, buckets, b, p, 2, p, (0,) if b < core else (core,))

    top = core - 1
    lean = core - 2 == 1
    sends_1 = bit[top] + 1 - bit[1]
    takes_1 = bit[top] + bit[1]

    def spread(p, n, i):
        where = rows_of(p)
        base = 3 * bits * heads
        return pltpu.make_async_remote_copy(
            src_ref=buckets.at[core, where], dst_ref=buckets.at[core, where],
            send_sem=send_sem.at[base + n * half + i], recv_sem=recv_sem.at[base + p],
            device_id=peer(targets[n]), device_id_type=MESH_ID,
        )

    def when_lean(b, amount, do):
        if b == 1 and lean:
            pl.when(amount > 0)(do)
        else:
            do()

    def when_top(b, do):
        if b == top:
            pl.when(bit[top] == 1)(do)
        else:
            do()

    def far_copy(b, p, n, m):
        return copy(sums, buckets, b, p, 0, n * (half // 2) + m, (b,) + targets[n])

    peers = [(b,) for b in (0, 1)] + [(b,) for b in range(1, core - 1) if b > 1] + [(b - 1, b) for b in range(2, core)]
    peers += [(0, core - 2), (core,)] + [(b,) + c for b in range(core + 1, bits) for c in targets]

    barrier = pltpu.get_barrier_semaphore()
    for flips in peers:
        pl.semaphore_signal(barrier, inc=1, device_id=peer(flips), device_id_type=MESH_ID)

    chunk = length // CHUNKS
    first_loads = []
    for c in range(CHUNKS):
        for n, (src, dst) in enumerate([(k_ref, k_in), (v_ref, v_in)]):
            at = pl.ds(c * chunk, chunk)
            first_loads.append(pltpu.make_async_copy(src.at[at], dst.at[at], load_sem.at[2 * c + n]))
    loads = [pltpu.make_async_copy(q_ref, q_in, load_sem.at[2 * CHUNKS])]
    for h in range(heads):
        loads.append(pltpu.make_async_copy(w_ref.at[:, h, :], w_in.at[h], load_sem.at[2 * CHUNKS + 1 + h]))
    for load in first_loads:
        load.start()

    part = 64

    def widen(src, dst, start, stop):
        def step(i, _):
            at = pl.multiple_of(i * part, part)
            x = src[pl.ds(at, part)].astype(jnp.float32)
            dst[pl.ds(pl.multiple_of(at * heads, part * heads), part * heads), :] = x.reshape(part * heads, width)
            return 0
        lax.fori_loop(start // part, stop // part, step, 0)

    for c in range(CHUNKS):
        for n, (src, dst) in enumerate([(k_in, wide_a), (v_in, wide_b)]):
            first_loads[2 * c + n].wait()
            if c == CHUNKS - 1 and n == 1:
                for load in loads:
                    load.start()
            widen(src, dst, c * chunk, (c + 1) * chunk)

    def state_step(i, _):
        h = (1 - bit[0] + i // half * (2 * bit[0] - 1)) * half + i % half
        key = wide_a[pl.ds(h, length, stride=heads), :].astype(jnp.bfloat16)
        turned = wide_b[pl.ds(h, length, stride=heads), :].T.astype(jnp.bfloat16)
        k_heads[h] = key
        v_turned[h] = turned
        sums[0, pl.ds(pl.multiple_of(h * width, width), width), :] = jnp.dot(turned, key, preferred_element_type=jnp.float32)

        @pl.when(i == 0)
        def _():
            pl.semaphore_wait(barrier, len(peers))

        cross(0, h).start()
        return 0

    lax.fori_loop(0, heads, state_step, 0)

    row = lax.broadcasted_iota(jnp.int32, (SUB, SUB), 0)
    col = lax.broadcasted_iota(jnp.int32, (SUB, SUB), 1)
    differ = jnp.bitwise_xor(row, col)
    table = jnp.zeros((SUB, SUB), jnp.int32)
    for b in range(log2(SUB)):
        table = table + (differ >= 1 << b).astype(jnp.int32)
    levels[...] = jnp.where(row <= col, table, -1)

    loads[0].wait()
    widen(q_in, wide_a, 0, length)
    for load in loads[1:]:
        load.wait()

    def near_head(h):
        q_heads[h] = wide_a[pl.ds(h, length, stride=heads), :].astype(jnp.bfloat16)
        level = levels[...]
        for ti in range(length // TILE):
            cols = pl.ds(ti * TILE, TILE)
            query = q_heads[h, cols, :]
            total = None
            for si in range(ti + 1):
                scores = nt_dot(k_heads[h, pl.ds(si * TILE, TILE), :], query)
                if si < ti:
                    weighted = scores * w_in[h, pl.ds(log2(TILE) + (ti ^ si).bit_length(), 1), cols]
                else:
                    columns = []
                    for a in range(TILE // SUB):
                        at = pl.ds(ti * TILE + a * SUB, SUB)
                        parts = []
                        for c in range(TILE // SUB):
                            block = scores[c * SUB : (c + 1) * SUB, a * SUB : (a + 1) * SUB]
                            if c < a:
                                parts.append(block * w_in[h, pl.ds(log2(SUB) + (a ^ c).bit_length(), 1), at])
                            elif c > a:
                                parts.append(jnp.zeros_like(block))
                            else:
                                mixing = jnp.zeros((SUB, SUB), jnp.float32)
                                for n in range(log2(SUB) + 1):
                                    mixing = jnp.where(level == n, w_in[h, pl.ds(n, 1), at], mixing)
                                parts.append(mixing * block)
                        columns.append(jnp.concatenate(parts, 0))
                    weighted = jnp.concatenate(columns, 1)
                product = jnp.dot(
                    v_turned[h, :, pl.ds(si * TILE, TILE)], weighted.astype(jnp.bfloat16),
                    preferred_element_type=jnp.float32,
                )
                total = product if total is None else total + product
            near[h, :, cols] = total

    def add_up(b, p):
        if b < bits - 1:
            where = rows_of(p)
            sums[b + 1, where, :] = sums[b, where, :] + buckets[b, where, :]

    def when_low(b, do):
        if b < bits - 1 and b != core:
            do()
        else:
            pl.when(bit[b] == 0)(do)

    def when_high(b, do):
        if b < bits - 1 and b != core:
            do()
        else:
            pl.when(bit[b] == 1)(do)

    def when_gateway(b, do, yes=1):
        pl.when(gateway(b) == yes)(do)

    def by_core(m, away=False):
        return 2 * m + (1 - bit[core] if away else bit[core])

    events = []
    free = {}

    def flight(link, ready, step, latency):
        end = max(free.get(link, 0), ready) + step
        free[link] = end
        return end + latency

    def event(at, do, *given):
        events.append((at, functools.partial(do, *given)))

    def begin(b, side, i):
        p = side(i)
        if b < 2:
            when_lean(b, sends_1, lambda: cross(b, p).start())
        elif b < core:
            if side is mine:
                when_gateway(b, lambda: cross(b, p).start())
        elif b == core:
            if side is mine:
                @pl.when(gateway(top) + 1 - bit[core] > 0)
                def _():
                    cross(b, p).start()
            else:
                when_low(b, lambda: cross(b, p).start())

    def arrived(b, side, i):
        def do():
            p = side(i)
            cross(b, p).wait_recv()
            add_up(b, p)
            begin(b + 1, side, i)
        when_lean(b, takes_1, do)

    def cross_arrived(b, i):
        def do():
            p = mine(i)
            cross(b, p).wait_recv()

            def on():
                relay(b, p).start()
                share(b, p).start()
            when_top(b, on)
            add_up(b, p)
            begin(b + 1, mine, i)
        when_gateway(b, do)

    def relay_arrived(b, i):
        def do():
            p = mine(i)
            relay(b, p).wait_recv()
            share(b, p).start()
            add_up(b, p)
            begin(b + 1, mine, i)
        when_gateway(b, lambda: when_top(b, do), 0)

    def share_arrived(b, yes, i):
        def do():
            p = other(i)
            share(b, p).wait_recv()
            add_up(b, p)
            begin(b + 1, other, i)
        when_gateway(b, lambda: when_top(b, do), yes)

    def core_pair(m):
        def do():
            for i in (2 * m, 2 * m + 1):
                cross(core, mine(i)).wait_recv()
            add_up(core, mine(by_core(m)))
            begin_far(core + 1, m)

            @pl.when((1 - bit[top]) * bit[core] == 1)
            def _():
                for i in (2 * m, 2 * m + 1):
                    for n in range(1, len(targets)):
                        spread(mine(i), n, i).start()
        when_gateway(top, do)

    def low_arrived(side, yes, i):
        @pl.when((1 - bit[top]) * bit[core] == 1)
        def _():
            when_gateway(top, lambda: spread(side(i), 0, i).wait_recv(), yes)

    def core_arrived(side, yes, i):
        def do():
            when_high(core, lambda: cross(core, side(i)).wait_recv())
        when_gateway(top, lambda: when_top(top, do), yes)

    def begin_far(b, m):
        def do():
            for n in range(len(targets)):
                far_copy(b, mine(by_core(m)), n, m).start()
        if b < bits:
            when_low(b, do)

    def far_arrived(b, side, m):
        p = side(by_core(m))

        def do():
            far_copy(b, p, 0, 0).wait_recv()
            share(b, p).start()
        when_high(b, do)
        if side is mine and b < bits - 1:
            def on():
                add_up(b, p)
                begin_far(b + 1, m)
            when_gateway(core - 1, on)

    def far_share_arrived(b, side, m):
        when_high(b, lambda: share(b, side(by_core(m, True))).wait_recv())

    when = {}
    for n, (side, i) in enumerate([(mine, i) for i in range(half)] + [(other, i) for i in range(half)]):
        when[side, i] = flight(0, STATE_TIME * (n + 1), STEP, LATENCY)
    for b in range(2):
        later = {}
        for (side, i), at in sorted(when.items(), key=lambda e: e[1]):
            event(at, arrived, b, side, i)
            later[side, i] = flight(1, at, STEP, LATENCY)
        if b == 0:
            when = later
    whole_at = dict(when)
    early = {}
    for b in range(2, core):
        later = {}
        for i in range(half):
            at = flight(("gate", b), when[mine, i], STEP, LATENCY)
            event(at, cross_arrived, b, i)
            early[i] = at
            near_share = max(flight(("share", b), at, STEP, LATENCY), when[other, i] + 0.01)
            event(near_share, share_arrived, b, 1, i)
            relayed = max(flight(("relay", b), at, STEP, LATENCY), when[mine, i] + 0.01)
            event(relayed, relay_arrived, b, i)
            last = max(flight(("last", b), relayed, STEP, LATENCY), when[other, i] + 0.01)
            event(last, share_arrived, b, 0, i)
            later[mine, i] = relayed
            later[other, i] = last
            if b == core - 1:
                event(near_share + CORE_LATENCY, core_arrived, other, 1, i)
                event(relayed + CORE_LATENCY, core_arrived, mine, 0, i)
                event(last + CORE_LATENCY, core_arrived, other, 0, i)
        when = later
    done = {i: max(when[mine, i], when[other, i]) + CORE_LATENCY for i in range(half)}
    for m in range(half // 2):
        at = early[2 * m + 1] + CORE_LATENCY
        event(at, core_pair, m)
        for i in (2 * m, 2 * m + 1):
            landed = flight("low", at, STEP, LATENCY + 0.5)
            event(landed, low_arrived, other, 1, i)
            event(landed, low_arrived, mine, 0, i)
            event(landed + 0.5, low_arrived, other, 0, i)
        for b in range(core + 1, bits):
            for side in (mine, other):
                landed = flight(b, at, STEP, LATENCY + 0.7)
                event(landed, far_arrived, b, side, m)
                event(landed + CORE_LATENCY, far_share_arrived, b, side, m)
            at = landed
            for i in (2 * m, 2 * m + 1):
                done[i] = max(done[i], landed + CORE_LATENCY)

    def far_head(h, chosen, last):
        where = pl.ds(pl.multiple_of(h * width, width), width)
        high = []
        low = []
        for b in chosen:
            whole = jnp.where(bit[b] == 1, buckets[b, where, :], 0.0)
            top = whole.astype(jnp.bfloat16)
            high.append(top)
            low.append((whole - top.astype(jnp.float32)).astype(jnp.bfloat16))
        both = jnp.concatenate([jnp.concatenate(high, 0), jnp.concatenate(low, 0)], 1)
        for ti in range(length // TILE):
            cols = pl.ds(ti * TILE, TILE)
            query = q_heads[h, cols, :]
            products = nt_dot(both, jnp.concatenate([query, query], 1))
            total = near[h, :, cols]
            for n, b in enumerate(chosen):
                total = total + products[n * width : (n + 1) * width] * w_in[h, pl.ds(local_bits + 1 + b, 1), cols]
            if last:
                scale = lax.rsqrt(jnp.mean(total * total, 0, keepdims=True) + EPSILON)
                wide_b[pl.ds(ti * TILE * heads + h, TILE, stride=heads), :] = (total * scale).T
            else:
                near[h, :, cols] = total

    first = [0, 1]
    last = list(range(2, bits))
    loops = [
        (heads, NEAR_TIME, [0] * heads, lambda i: near_head(i)),
        (half, 0.43, [whole_at[mine, i] for i in range(half)], lambda i: far_head(mine(i), first, False)),
        (half, 0.43, [whole_at[other, i] for i in range(half)], lambda i: far_head(other(i), first, False)),
        (half, 1.2, [done[i] for i in range(half)], lambda i: (far_head(mine(i), last, True), far_head(other(i), last, True))),
    ]
    waiting = sorted(events, key=lambda e: e[0])
    clock = STATE_TIME * heads
    for count, cost, needs, work in loops:
        slots = []
        for need in needs:
            slots.append([])
            while waiting and waiting[0][0] <= max(clock, need + 0.02):
                at, do = waiting.pop(0)
                slots[-1].append(do)
                clock = max(clock, at)
            clock += cost

        def one(i, _, slots=slots, work=work):
            for at, group in enumerate(slots):
                def run(group=group):
                    for do in group:
                        do()
                if group:
                    pl.when(i == at)(run)
            work(i)
            return 0

        lax.fori_loop(0, count, one, 0)
    assert not waiting

    def sent(i, _):
        for side in (mine, other):
            p = side(i)
            cross(0, p).wait_send()
            when_lean(1, sends_1, lambda: cross(1, p).wait_send())
            amount = (1 - bit[core]) * bit[top]
            if side is mine:
                amount = amount + gateway(top)

            @pl.when(amount > 0)
            def _():
                cross(core, p).wait_send()
        for b in range(2, core):
            when_top(b, lambda: share(b, mine(i)).wait_send())

            def do():
                cross(b, mine(i)).wait_send()
                when_top(b, lambda: relay(b, mine(i)).wait_send())
            when_gateway(b, do)

        @pl.when((1 - bit[top]) * bit[core] * gateway(top) == 1)
        def _():
            for n in range(1, len(targets)):
                spread(mine(i), n, i).wait_send()
        return 0

    lax.fori_loop(0, half, sent, 0)

    def far_sent(m, _):
        for b in range(core + 1, bits):
            def do():
                for n in range(len(targets)):
                    far_copy(b, mine(by_core(m)), n, m).wait_send()
            when_gateway(core - 1, lambda: when_low(b, do))

            def do_share():
                for side in (mine, other):
                    share(b, side(by_core(m))).wait_send()
            when_high(b, do_share)
        return 0

    lax.fori_loop(0, half // 2, far_sent, 0)


def per_device(query, key, value, level_weight):
    length, heads, width = query.shape
    short_bits = log2(lax.axis_size("short"))
    long_bits = log2(lax.axis_size("long"))
    bits = short_bits + long_bits
    rows = heads * width
    copies = 3 * bits * heads + 2 * heads
    level_weight = jnp.transpose(level_weight, (1, 0, 2))
    total = pl.pallas_call(
        functools.partial(kernel, short_bits, long_bits, heads, length, width),
        out_shape=pltpu.VMEM((length * heads, width), jnp.float32),
        in_specs=[pl.BlockSpec(memory_space=pl.ANY)] * 4,
        out_specs=pl.BlockSpec(memory_space=pltpu.VMEM),
        scratch_shapes=[
            pltpu.VMEM(query.shape, jnp.bfloat16),
            pltpu.VMEM(query.shape, jnp.bfloat16),
            pltpu.VMEM(query.shape, jnp.bfloat16),
            pltpu.VMEM((heads, level_weight.shape[0], length), jnp.float32),
            pltpu.VMEM((length * heads, width), jnp.float32),
            pltpu.VMEM((heads, length, width), jnp.bfloat16),
            pltpu.VMEM((heads, length, width), jnp.bfloat16),
            pltpu.VMEM((heads, width, length), jnp.bfloat16),
            pltpu.VMEM((heads, width, length), jnp.float32),
            pltpu.VMEM((SUB, SUB), jnp.int32),
            pltpu.VMEM((bits, rows, width), jnp.float32),
            pltpu.VMEM((bits, rows, width), jnp.float32),
            pltpu.SemaphoreType.DMA((copies,)),
            pltpu.SemaphoreType.DMA((copies,)),
            pltpu.SemaphoreType.DMA((2 * CHUNKS + 1 + heads,)),
        ],
        compiler_params=pltpu.CompilerParams(
            collective_id=0, has_side_effects=True, vmem_limit_bytes=52 * 1024 * 1024
        ),
    )(query, key, value, level_weight)
    return total.reshape(query.shape).astype(jnp.bfloat16)


def solution(mesh):
    rows = P(("long", "short"), None)
    return jax.shard_map(
        per_device,
        mesh=mesh,
        in_specs=(rows, rows, rows, P(None, None, ("long", "short"))),
        out_specs=rows,
        check_vma=False,
    )
```

```python
import functools

import jax
import jax.numpy as jnp
from jax import lax
from jax.experimental import pallas as pl
from jax.experimental.pallas import tpu as pltpu
from jax.sharding import PartitionSpec as P

EPSILON = 1e-06
TILE = 256
NEAR_TILE = 512
SUB = 128
STATE_TIME = 0.43
NEAR_TIME = 0.95
STEP = 1.31
LATENCY = 2.4
CORE_LATENCY = 1.0
CHUNKS = 4
MESH_ID = pl.DeviceIdType.MESH


def log2(n):
    return n.bit_length() - 1


def subsets(bits):
    found = [tuple(b for i, b in enumerate(bits) if mask >> i & 1) for mask in range(1 << len(bits))]
    return sorted(found, key=len)


def nt_dot(a, b):
    return lax.dot_general(a, b, (((1,), (1,)), ((), ())), preferred_element_type=jnp.float32)


def kernel(
    short_bits, long_bits, heads, length, width,
    q_ref, k_ref, v_ref, w_ref, wide_b,
    k_in, v_in, q_in, w_in, wide_a, q_heads, k_heads, v_turned, near, levels, sums, buckets, send_sem, recv_sem, load_sem,
):
    bits = short_bits + long_bits
    rows = heads * width
    local_bits = log2(length)
    short_pos = lax.axis_index("short")
    long_pos = lax.axis_index("long")
    bit = [(short_pos // (1 << b)) % 2 for b in range(short_bits)]
    bit += [(long_pos // (1 << b)) % 2 for b in range(long_bits)]

    core = short_bits
    half = heads // 2
    targets = subsets([0, core - 2])

    def gateway(b):
        return bit[b - 1] + bit[b] - 2 * bit[b - 1] * bit[b]

    def peer(flips):
        short = short_pos
        long = long_pos
        for b in flips:
            if b < short_bits:
                short = short + (1 - 2 * bit[b]) * (1 << b)
            else:
                long = long + (1 - 2 * bit[b]) * (1 << b - short_bits)
        return {"short": short, "long": long}

    def mine(i):
        return bit[0] * half + i

    def other(i):
        return (1 - bit[0]) * half + i

    def rows_of(p):
        return pl.ds(pl.multiple_of(p * width, width), width)

    def copy(src, dst, b, p, bank, sent, to):
        where = rows_of(p)
        base = (3 * b + bank) * heads
        return pltpu.make_async_remote_copy(
            src_ref=src.at[b, where], dst_ref=dst.at[b, where],
            send_sem=send_sem.at[base + sent], recv_sem=recv_sem.at[base + p],
            device_id=peer(to), device_id_type=MESH_ID,
        )

    def cross(b, p):
        return copy(sums, buckets, b, p, 0, p, (b,) if b < 2 or b >= core else (b - 1, b))

    def relay(b, p):
        return copy(buckets, buckets, b, p, 1, p, (b - 1,))

    def share(b, p):
        return copy(buckets, buckets, b, p, 2, p, (0,) if b < core else (core,))

    top = core - 1
    lean = core - 2 == 1
    sends_1 = bit[top] + 1 - bit[1]
    takes_1 = bit[top] + bit[1]

    def spread(p, n, i):
        where = rows_of(p)
        base = 3 * bits * heads
        return pltpu.make_async_remote_copy(
            src_ref=buckets.at[core, where], dst_ref=buckets.at[core, where],
            send_sem=send_sem.at[base + n * half + i], recv_sem=recv_sem.at[base + p],
            device_id=peer(targets[n]), device_id_type=MESH_ID,
        )

    def when_lean(b, amount, do):
        if b == 1 and lean:
            pl.when(amount > 0)(do)
        else:
            do()

    def when_top(b, do):
        if b == top:
            pl.when(bit[top] == 1)(do)
        else:
            do()

    def far_copy(b, p, n, m):
        return copy(sums, buckets, b, p, 0, n * (half // 2) + m, (b,) + targets[n])

    peers = [(b,) for b in (0, 1)] + [(b,) for b in range(1, core - 1) if b > 1] + [(b - 1, b) for b in range(2, core)]
    peers += [(0, core - 2), (core,)] + [(b,) + c for b in range(core + 1, bits) for c in targets]

    barrier = pltpu.get_barrier_semaphore()
    for flips in peers:
        pl.semaphore_signal(barrier, inc=1, device_id=peer(flips), device_id_type=MESH_ID)

    chunk = length // CHUNKS
    first_loads = []
    for c in range(CHUNKS):
        for n, (src, dst) in enumerate([(k_ref, k_in), (v_ref, v_in)]):
            at = pl.ds(c * chunk, chunk)
            first_loads.append(pltpu.make_async_copy(src.at[at], dst.at[at], load_sem.at[2 * c + n]))
    loads = [pltpu.make_async_copy(q_ref, q_in, load_sem.at[2 * CHUNKS])]
    for h in range(heads):
        loads.append(pltpu.make_async_copy(w_ref.at[:, h, :], w_in.at[h], load_sem.at[2 * CHUNKS + 1 + h]))
    for load in first_loads:
        load.start()

    part = 64

    def widen(src, dst, start, stop):
        def step(i, _):
            at = pl.multiple_of(i * part, part)
            x = src[pl.ds(at, part)].astype(jnp.float32)
            dst[pl.ds(pl.multiple_of(at * heads, part * heads), part * heads), :] = x.reshape(part * heads, width)
            return 0
        lax.fori_loop(start // part, stop // part, step, 0)

    for c in range(CHUNKS):
        for n, (src, dst) in enumerate([(k_in, wide_a), (v_in, wide_b)]):
            first_loads[2 * c + n].wait()
            if c == CHUNKS - 1 and n == 1:
                for load in loads:
                    load.start()
            widen(src, dst, c * chunk, (c + 1) * chunk)

    def state_step(i, _):
        h = (1 - bit[0] + i // half * (2 * bit[0] - 1)) * half + i % half
        key = wide_a[pl.ds(h, length, stride=heads), :].astype(jnp.bfloat16)
        turned = wide_b[pl.ds(h, length, stride=heads), :].T.astype(jnp.bfloat16)
        k_heads[h] = key
        v_turned[h] = turned
        sums[0, pl.ds(pl.multiple_of(h * width, width), width), :] = jnp.dot(turned, key, preferred_element_type=jnp.float32)

        @pl.when(i == 0)
        def _():
            pl.semaphore_wait(barrier, len(peers))

        cross(0, h).start()
        return 0

    lax.fori_loop(0, heads, state_step, 0)

    row = lax.broadcasted_iota(jnp.int32, (SUB, SUB), 0)
    col = lax.broadcasted_iota(jnp.int32, (SUB, SUB), 1)
    differ = jnp.bitwise_xor(row, col)
    table = jnp.zeros((SUB, SUB), jnp.int32)
    for b in range(log2(SUB)):
        table = table + (differ >= 1 << b).astype(jnp.int32)
    levels[...] = jnp.where(row <= col, table, -1)

    loads[0].wait()
    widen(q_in, wide_a, 0, length)
    for load in loads[1:]:
        load.wait()

    def near_head(h):
        q_heads[h] = wide_a[pl.ds(h, length, stride=heads), :].astype(jnp.bfloat16)
        level = levels[...]
        for ti in range(length // NEAR_TILE):
            cols = pl.ds(ti * NEAR_TILE, NEAR_TILE)
            query = q_heads[h, cols, :]
            pieces = []
            for si in range(ti + 1):
                scores = nt_dot(k_heads[h, pl.ds(si * NEAR_TILE, NEAR_TILE), :], query)
                if si < ti:
                    weighted = scores * w_in[h, pl.ds(log2(NEAR_TILE) + (ti ^ si).bit_length(), 1), cols]
                else:
                    columns = []
                    for a in range(NEAR_TILE // SUB):
                        at = pl.ds(ti * NEAR_TILE + a * SUB, SUB)
                        parts = []
                        for c in range(NEAR_TILE // SUB):
                            block = scores[c * SUB : (c + 1) * SUB, a * SUB : (a + 1) * SUB]
                            if c < a:
                                parts.append(block * w_in[h, pl.ds(log2(SUB) + (a ^ c).bit_length(), 1), at])
                            elif c > a:
                                parts.append(jnp.zeros_like(block))
                            else:
                                mixing = jnp.zeros((SUB, SUB), jnp.float32)
                                for n in range(log2(SUB) + 1):
                                    mixing = jnp.where(level == n, w_in[h, pl.ds(n, 1), at], mixing)
                                parts.append(mixing * block)
                        columns.append(jnp.concatenate(parts, 0))
                    weighted = jnp.concatenate(columns, 1)
                pieces.append(weighted.astype(jnp.bfloat16))
            near[h, :, cols] = jnp.dot(
                v_turned[h, :, pl.ds(0, (ti + 1) * NEAR_TILE)], jnp.concatenate(pieces, 0),
                preferred_element_type=jnp.float32,
            )

    def add_up(b, p):
        if b < bits - 1:
            where = rows_of(p)
            sums[b + 1, where, :] = sums[b, where, :] + buckets[b, where, :]

    def when_low(b, do):
        if b < bits - 1 and b != core:
            do()
        else:
            pl.when(bit[b] == 0)(do)

    def when_high(b, do):
        if b < bits - 1 and b != core:
            do()
        else:
            pl.when(bit[b] == 1)(do)

    def when_gateway(b, do, yes=1):
        pl.when(gateway(b) == yes)(do)

    def by_core(m, away=False):
        return 2 * m + (1 - bit[core] if away else bit[core])

    events = []
    free = {}

    def flight(link, ready, step, latency):
        end = max(free.get(link, 0), ready) + step
        free[link] = end
        return end + latency

    def event(at, do, *given):
        events.append((at, functools.partial(do, *given)))

    def begin(b, side, i):
        p = side(i)
        if b < 2:
            when_lean(b, sends_1, lambda: cross(b, p).start())
        elif b < core:
            if side is mine:
                when_gateway(b, lambda: cross(b, p).start())
        elif b == core:
            if side is mine:
                @pl.when(gateway(top) + 1 - bit[core] > 0)
                def _():
                    cross(b, p).start()
            else:
                when_low(b, lambda: cross(b, p).start())

    def arrived(b, side, i):
        def do():
            p = side(i)
            cross(b, p).wait_recv()
            add_up(b, p)
            begin(b + 1, side, i)
        when_lean(b, takes_1, do)

    def cross_arrived(b, i):
        def do():
            p = mine(i)
            cross(b, p).wait_recv()

            def on():
                relay(b, p).start()
                share(b, p).start()
            when_top(b, on)
            add_up(b, p)
            begin(b + 1, mine, i)
        when_gateway(b, do)

    def relay_arrived(b, i):
        def do():
            p = mine(i)
            relay(b, p).wait_recv()
            share(b, p).start()
            add_up(b, p)
            begin(b + 1, mine, i)
        when_gateway(b, lambda: when_top(b, do), 0)

    def share_arrived(b, yes, i):
        def do():
            p = other(i)
            share(b, p).wait_recv()
            add_up(b, p)
            begin(b + 1, other, i)
        when_gateway(b, lambda: when_top(b, do), yes)

    def core_pair(m):
        def do():
            for i in (2 * m, 2 * m + 1):
                cross(core, mine(i)).wait_recv()
            add_up(core, mine(by_core(m)))
            begin_far(core + 1, m)

            @pl.when((1 - bit[top]) * bit[core] == 1)
            def _():
                for i in (2 * m, 2 * m + 1):
                    for n in range(1, len(targets)):
                        spread(mine(i), n, i).start()
        when_gateway(top, do)

    def low_arrived(side, yes, i):
        @pl.when((1 - bit[top]) * bit[core] == 1)
        def _():
            when_gateway(top, lambda: spread(side(i), 0, i).wait_recv(), yes)

    def core_arrived(side, yes, i):
        def do():
            when_high(core, lambda: cross(core, side(i)).wait_recv())
        when_gateway(top, lambda: when_top(top, do), yes)

    def begin_far(b, m):
        def do():
            for n in range(len(targets)):
                far_copy(b, mine(by_core(m)), n, m).start()
        if b < bits:
            when_low(b, do)

    def far_arrived(b, side, m):
        p = side(by_core(m))

        def do():
            far_copy(b, p, 0, 0).wait_recv()
            share(b, p).start()
        when_high(b, do)
        if side is mine and b < bits - 1:
            def on():
                add_up(b, p)
                begin_far(b + 1, m)
            when_gateway(core - 1, on)

    def far_share_arrived(b, side, m):
        when_high(b, lambda: share(b, side(by_core(m, True))).wait_recv())

    when = {}
    for n, (side, i) in enumerate([(mine, i) for i in range(half)] + [(other, i) for i in range(half)]):
        when[side, i] = flight(0, STATE_TIME * (n + 1), STEP, LATENCY)
    for b in range(2):
        later = {}
        for (side, i), at in sorted(when.items(), key=lambda e: e[1]):
            event(at, arrived, b, side, i)
            later[side, i] = flight(1, at, STEP, LATENCY)
        if b == 0:
            when = later
    whole_at = dict(when)
    early = {}
    for b in range(2, core):
        later = {}
        for i in range(half):
            at = flight(("gate", b), when[mine, i], STEP, LATENCY)
            event(at, cross_arrived, b, i)
            early[i] = at
            near_share = max(flight(("share", b), at, STEP, LATENCY), when[other, i] + 0.01)
            event(near_share, share_arrived, b, 1, i)
            relayed = max(flight(("relay", b), at, STEP, LATENCY), when[mine, i] + 0.01)
            event(relayed, relay_arrived, b, i)
            last = max(flight(("last", b), relayed, STEP, LATENCY), when[other, i] + 0.01)
            event(last, share_arrived, b, 0, i)
            later[mine, i] = relayed
            later[other, i] = last
            if b == core - 1:
                event(near_share + CORE_LATENCY, core_arrived, other, 1, i)
                event(relayed + CORE_LATENCY, core_arrived, mine, 0, i)
                event(last + CORE_LATENCY, core_arrived, other, 0, i)
        when = later
    done = {i: max(when[mine, i], when[other, i]) + CORE_LATENCY for i in range(half)}
    for m in range(half // 2):
        at = early[2 * m + 1] + CORE_LATENCY
        event(at, core_pair, m)
        for i in (2 * m, 2 * m + 1):
            landed = flight("low", at, STEP, LATENCY + 0.5)
            event(landed, low_arrived, other, 1, i)
            event(landed, low_arrived, mine, 0, i)
            event(landed + 0.5, low_arrived, other, 0, i)
        for b in range(core + 1, bits):
            for side in (mine, other):
                landed = flight(b, at, STEP, LATENCY + 0.7)
                event(landed, far_arrived, b, side, m)
                event(landed + CORE_LATENCY, far_share_arrived, b, side, m)
            at = landed
            for i in (2 * m, 2 * m + 1):
                done[i] = max(done[i], landed + CORE_LATENCY)

    def far_head(h, chosen, last):
        where = pl.ds(pl.multiple_of(h * width, width), width)
        high = []
        low = []
        for b in chosen:
            whole = jnp.where(bit[b] == 1, buckets[b, where, :], 0.0)
            top = whole.astype(jnp.bfloat16)
            high.append(top)
            low.append((whole - top.astype(jnp.float32)).astype(jnp.bfloat16))
        both = jnp.concatenate([jnp.concatenate(high, 0), jnp.concatenate(low, 0)], 1)
        for ti in range(length // TILE):
            cols = pl.ds(ti * TILE, TILE)
            query = q_heads[h, cols, :]
            products = nt_dot(both, jnp.concatenate([query, query], 1))
            total = near[h, :, cols]
            for n, b in enumerate(chosen):
                total = total + products[n * width : (n + 1) * width] * w_in[h, pl.ds(local_bits + 1 + b, 1), cols]
            if last:
                scale = lax.rsqrt(jnp.mean(total * total, 0, keepdims=True) + EPSILON)
                wide_b[pl.ds(ti * TILE * heads + h, TILE, stride=heads), :] = (total * scale).T
            else:
                near[h, :, cols] = total

    first = [0, 1]
    last = list(range(2, bits))
    loops = [
        (heads, NEAR_TIME, [0] * heads, lambda i: near_head(i)),
        (
            half // 2, 0.66, [whole_at[mine, 2 * i + 1] for i in range(half // 2)],
            lambda i: (far_head(mine(2 * i), first, False), far_head(mine(2 * i + 1), first, False)),
        ),
        (
            half // 2, 0.66, [whole_at[other, 2 * i + 1] for i in range(half // 2)],
            lambda i: (far_head(other(2 * i), first, False), far_head(other(2 * i + 1), first, False)),
        ),
        (half, 0.7, [done[i] for i in range(half)], lambda i: (far_head(mine(i), last, True), far_head(other(i), last, True))),
    ]
    waiting = sorted(events, key=lambda e: e[0])
    clock = STATE_TIME * heads
    for count, cost, needs, work in loops:
        slots = []
        for need in needs:
            slots.append([])
            while waiting and waiting[0][0] <= max(clock, need + 0.02):
                at, do = waiting.pop(0)
                slots[-1].append(do)
                clock = max(clock, at)
            clock += cost

        def one(i, _, slots=slots, work=work):
            for at, group in enumerate(slots):
                def run(group=group):
                    for do in group:
                        do()
                if group:
                    pl.when(i == at)(run)
            work(i)
            return 0

        lax.fori_loop(0, count, one, 0)
    assert not waiting

    def sent(i, _):
        for side in (mine, other):
            p = side(i)
            cross(0, p).wait_send()
            when_lean(1, sends_1, lambda: cross(1, p).wait_send())
            amount = (1 - bit[core]) * bit[top]
            if side is mine:
                amount = amount + gateway(top)

            @pl.when(amount > 0)
            def _():
                cross(core, p).wait_send()
        for b in range(2, core):
            when_top(b, lambda: share(b, mine(i)).wait_send())

            def do():
                cross(b, mine(i)).wait_send()
                when_top(b, lambda: relay(b, mine(i)).wait_send())
            when_gateway(b, do)

        @pl.when((1 - bit[top]) * bit[core] * gateway(top) == 1)
        def _():
            for n in range(1, len(targets)):
                spread(mine(i), n, i).wait_send()
        return 0

    lax.fori_loop(0, half, sent, 0)

    def far_sent(m, _):
        for b in range(core + 1, bits):
            def do():
                for n in range(len(targets)):
                    far_copy(b, mine(by_core(m)), n, m).wait_send()
            when_gateway(core - 1, lambda: when_low(b, do))

            def do_share():
                for side in (mine, other):
                    share(b, side(by_core(m))).wait_send()
            when_high(b, do_share)
        return 0

    lax.fori_loop(0, half // 2, far_sent, 0)


def per_device(query, key, value, level_weight):
    length, heads, width = query.shape
    short_bits = log2(lax.axis_size("short"))
    long_bits = log2(lax.axis_size("long"))
    bits = short_bits + long_bits
    rows = heads * width
    copies = 3 * bits * heads + 2 * heads
    level_weight = jnp.transpose(level_weight, (1, 0, 2))
    total = pl.pallas_call(
        functools.partial(kernel, short_bits, long_bits, heads, length, width),
        out_shape=pltpu.VMEM((length * heads, width), jnp.float32),
        in_specs=[pl.BlockSpec(memory_space=pl.ANY)] * 4,
        out_specs=pl.BlockSpec(memory_space=pltpu.VMEM),
        scratch_shapes=[
            pltpu.VMEM(query.shape, jnp.bfloat16),
            pltpu.VMEM(query.shape, jnp.bfloat16),
            pltpu.VMEM(query.shape, jnp.bfloat16),
            pltpu.VMEM((heads, level_weight.shape[0], length), jnp.float32),
            pltpu.VMEM((length * heads, width), jnp.float32),
            pltpu.VMEM((heads, length, width), jnp.bfloat16),
            pltpu.VMEM((heads, length, width), jnp.bfloat16),
            pltpu.VMEM((heads, width, length), jnp.bfloat16),
            pltpu.VMEM((heads, width, length), jnp.float32),
            pltpu.VMEM((SUB, SUB), jnp.int32),
            pltpu.VMEM((bits, rows, width), jnp.float32),
            pltpu.VMEM((bits, rows, width), jnp.float32),
            pltpu.SemaphoreType.DMA((copies,)),
            pltpu.SemaphoreType.DMA((copies,)),
            pltpu.SemaphoreType.DMA((2 * CHUNKS + 1 + heads,)),
        ],
        compiler_params=pltpu.CompilerParams(
            collective_id=0, has_side_effects=True, vmem_limit_bytes=52 * 1024 * 1024
        ),
    )(query, key, value, level_weight)
    return total.reshape(query.shape).astype(jnp.bfloat16)


def solution(mesh):
    rows = P(("long", "short"), None)
    return jax.shard_map(
        per_device,
        mesh=mesh,
        in_specs=(rows, rows, rows, P(None, None, ("long", "short"))),
        out_specs=rows,
        check_vma=False,
    )
```

```python
import functools

import jax
import jax.numpy as jnp
from jax import lax
from jax.experimental import pallas as pl
from jax.experimental.pallas import tpu as pltpu
from jax.sharding import PartitionSpec as P

EPSILON = 1e-06
TILE = 256
NEAR_TILE = 512
SUB = 128
STATE_TIME = 0.43
NEAR_TIME = 0.95
STEP = 1.31
LATENCY = 2.4
CORE_LATENCY = 1.0
CHUNKS = 4
MESH_ID = pl.DeviceIdType.MESH


def log2(n):
    return n.bit_length() - 1


def subsets(bits):
    found = [tuple(b for i, b in enumerate(bits) if mask >> i & 1) for mask in range(1 << len(bits))]
    return sorted(found, key=len)


def nt_dot(a, b):
    return lax.dot_general(a, b, (((1,), (1,)), ((), ())), preferred_element_type=jnp.float32)


def kernel(
    short_bits, long_bits, heads, length, width,
    q_ref, k_ref, v_ref, w_ref, wide_b,
    k_in, v_in, q_in, w_in, wide_a, q_heads, k_heads, v_turned, near, levels, sums, buckets, send_sem, recv_sem, load_sem,
):
    bits = short_bits + long_bits
    rows = heads * width
    local_bits = log2(length)
    short_pos = lax.axis_index("short")
    long_pos = lax.axis_index("long")
    bit = [(short_pos // (1 << b)) % 2 for b in range(short_bits)]
    bit += [(long_pos // (1 << b)) % 2 for b in range(long_bits)]

    core = short_bits
    half = heads // 2
    targets = subsets([0, core - 2])

    def gateway(b):
        return bit[b - 1] + bit[b] - 2 * bit[b - 1] * bit[b]

    def peer(flips):
        short = short_pos
        long = long_pos
        for b in flips:
            if b < short_bits:
                short = short + (1 - 2 * bit[b]) * (1 << b)
            else:
                long = long + (1 - 2 * bit[b]) * (1 << b - short_bits)
        return {"short": short, "long": long}

    def mine(i):
        return bit[0] * half + i

    def other(i):
        return (1 - bit[0]) * half + i

    def rows_of(p):
        return pl.ds(pl.multiple_of(p * width, width), width)

    def copy(src, dst, b, p, bank, sent, to):
        where = rows_of(p)
        base = (3 * b + bank) * heads
        return pltpu.make_async_remote_copy(
            src_ref=src.at[b, where], dst_ref=dst.at[b, where],
            send_sem=send_sem.at[base + sent], recv_sem=recv_sem.at[base + p],
            device_id=peer(to), device_id_type=MESH_ID,
        )

    def cross(b, p):
        return copy(sums, buckets, b, p, 0, p, (b,) if b < 2 or b >= core else (b - 1, b))

    def relay(b, p):
        return copy(buckets, buckets, b, p, 1, p, (b - 1,))

    def share(b, p):
        return copy(buckets, buckets, b, p, 2, p, (0,) if b < core else (core,))

    top = core - 1
    lean = core - 2 == 1
    sends_1 = bit[top] + 1 - bit[1]
    takes_1 = bit[top] + bit[1]

    def spread(p, n, i):
        where = rows_of(p)
        base = 3 * bits * heads
        return pltpu.make_async_remote_copy(
            src_ref=buckets.at[core, where], dst_ref=buckets.at[core, where],
            send_sem=send_sem.at[base + n * half + i], recv_sem=recv_sem.at[base + p],
            device_id=peer(targets[n]), device_id_type=MESH_ID,
        )

    def when_lean(b, amount, do):
        if b == 1 and lean:
            pl.when(amount > 0)(do)
        else:
            do()

    def when_top(b, do):
        if b == top:
            pl.when(bit[top] == 1)(do)
        else:
            do()

    def far_copy(b, p, n, m):
        return copy(sums, buckets, b, p, 0, n * (half // 2) + m, (b,) + targets[n])

    peers = [(b,) for b in (0, 1)] + [(b,) for b in range(1, core - 1) if b > 1] + [(b - 1, b) for b in range(2, core)]
    peers += [(0, core - 2), (core,)] + [(b,) + c for b in range(core + 1, bits) for c in targets]

    barrier = pltpu.get_barrier_semaphore()
    for flips in peers:
        pl.semaphore_signal(barrier, inc=1, device_id=peer(flips), device_id_type=MESH_ID)

    chunk = length // CHUNKS
    first_loads = []
    for c in range(CHUNKS):
        for n, (src, dst) in enumerate([(k_ref, k_in), (v_ref, v_in)]):
            at = pl.ds(c * chunk, chunk)
            first_loads.append(pltpu.make_async_copy(src.at[at], dst.at[at], load_sem.at[2 * c + n]))
    loads = [pltpu.make_async_copy(q_ref, q_in, load_sem.at[2 * CHUNKS])]
    for h in range(heads):
        loads.append(pltpu.make_async_copy(w_ref.at[:, h, :], w_in.at[h], load_sem.at[2 * CHUNKS + 1 + h]))
    for load in first_loads:
        load.start()

    part = 64

    def widen(src, dst, start, stop):
        def step(i, _):
            at = pl.multiple_of(i * part, part)
            x = src[pl.ds(at, part)].astype(jnp.float32)
            dst[pl.ds(pl.multiple_of(at * heads, part * heads), part * heads), :] = x.reshape(part * heads, width)
            return 0
        lax.fori_loop(start // part, stop // part, step, 0)

    for c in range(CHUNKS):
        for n, (src, dst) in enumerate([(k_in, wide_a), (v_in, wide_b)]):
            first_loads[2 * c + n].wait()
            if c == CHUNKS - 1 and n == 1:
                for load in loads:
                    load.start()
            widen(src, dst, c * chunk, (c + 1) * chunk)

    def state_step(i, _):
        h = (1 - bit[0] + i // half * (2 * bit[0] - 1)) * half + i % half
        key = wide_a[pl.ds(h, length, stride=heads), :].astype(jnp.bfloat16)
        turned = wide_b[pl.ds(h, length, stride=heads), :].T.astype(jnp.bfloat16)
        k_heads[h] = key
        v_turned[h] = turned
        sums[0, pl.ds(pl.multiple_of(h * width, width), width), :] = jnp.dot(turned, key, preferred_element_type=jnp.float32)

        @pl.when(i == 0)
        def _():
            pl.semaphore_wait(barrier, len(peers))

        cross(0, h).start()
        return 0

    lax.fori_loop(0, heads, state_step, 0)

    row = lax.broadcasted_iota(jnp.int32, (SUB, SUB), 0)
    col = lax.broadcasted_iota(jnp.int32, (SUB, SUB), 1)
    differ = jnp.bitwise_xor(row, col)
    table = jnp.zeros((SUB, SUB), jnp.int32)
    for b in range(log2(SUB)):
        table = table + (differ >= 1 << b).astype(jnp.int32)
    levels[...] = jnp.where(row <= col, table, -1)

    loads[0].wait()
    widen(q_in, wide_a, 0, length)
    for load in loads[1:]:
        load.wait()

    def near_head(h):
        q_heads[h] = wide_a[pl.ds(h, length, stride=heads), :].astype(jnp.bfloat16)
        level = levels[...]
        for ti in range(length // NEAR_TILE):
            cols = pl.ds(ti * NEAR_TILE, NEAR_TILE)
            query = q_heads[h, cols, :]
            pieces = []
            for si in range(ti + 1):
                scores = nt_dot(k_heads[h, pl.ds(si * NEAR_TILE, NEAR_TILE), :], query)
                if si < ti:
                    weighted = scores * w_in[h, pl.ds(log2(NEAR_TILE) + (ti ^ si).bit_length(), 1), cols]
                else:
                    columns = []
                    for a in range(NEAR_TILE // SUB):
                        at = pl.ds(ti * NEAR_TILE + a * SUB, SUB)
                        parts = []
                        for c in range(NEAR_TILE // SUB):
                            block = scores[c * SUB : (c + 1) * SUB, a * SUB : (a + 1) * SUB]
                            if c < a:
                                parts.append(block * w_in[h, pl.ds(log2(SUB) + (a ^ c).bit_length(), 1), at])
                            elif c > a:
                                parts.append(jnp.zeros_like(block))
                            else:
                                mixing = jnp.zeros((SUB, SUB), jnp.float32)
                                for n in range(log2(SUB) + 1):
                                    mixing = jnp.where(level == n, w_in[h, pl.ds(n, 1), at], mixing)
                                parts.append(mixing * block)
                        columns.append(jnp.concatenate(parts, 0))
                    weighted = jnp.concatenate(columns, 1)
                pieces.append(weighted.astype(jnp.bfloat16))
            near[h, :, cols] = jnp.dot(
                v_turned[h, :, pl.ds(0, (ti + 1) * NEAR_TILE)], jnp.concatenate(pieces, 0),
                preferred_element_type=jnp.float32,
            )

    def add_up(b, p):
        if b < bits - 1:
            where = rows_of(p)
            sums[b + 1, where, :] = sums[b, where, :] + buckets[b, where, :]

    def when_low(b, do):
        if b < bits - 1 and b != core:
            do()
        else:
            pl.when(bit[b] == 0)(do)

    def when_high(b, do):
        if b < bits - 1 and b != core:
            do()
        else:
            pl.when(bit[b] == 1)(do)

    def when_gateway(b, do, yes=1):
        pl.when(gateway(b) == yes)(do)

    def by_core(m, away=False):
        return 2 * m + (1 - bit[core] if away else bit[core])

    events = []
    free = {}

    def flight(link, ready, step, latency):
        end = max(free.get(link, 0), ready) + step
        free[link] = end
        return end + latency

    def event(at, do, *given):
        events.append((at, functools.partial(do, *given)))

    outer = (1 - gateway(top)) * bit[top]

    def held_back(b, side, i):
        return lean and b == 1 and side is other and i >= half // 2

    def begin(b, side, i):
        p = side(i)
        if b < 2:
            go = sends_1
            if held_back(b, side, i):
                go = go * (1 - bit[top] * gateway(top))
            when_lean(b, go, lambda: cross(b, p).start())
        elif b < core:
            if side is mine:
                when_gateway(b, lambda: cross(b, p).start())
        elif b == core:
            if side is mine:
                cross(b, p).start()
            else:
                when_low(b, lambda: cross(b, p).start())

    def arrived(b, side, i, kind=None):
        def do():
            p = side(i)
            cross(b, p).wait_recv()
            add_up(b, p)
            begin(b + 1, side, i)
        if kind is None:
            when_lean(b, takes_1, do)
        else:
            pl.when(takes_1 * (1 - outer if kind == 0 else outer) > 0)(do)

    def cross_arrived(b, i):
        def do():
            p = mine(i)
            cross(b, p).wait_recv()

            def on():
                relay(b, p).start()
                share(b, p).start()
                if b == top and held_back(1, other, i):
                    cross(1, other(i)).start()
            when_top(b, on)
            add_up(b, p)
            begin(b + 1, mine, i)
        when_gateway(b, do)

    def relay_arrived(b, i):
        def do():
            p = mine(i)
            relay(b, p).wait_recv()
            share(b, p).start()
            add_up(b, p)
            begin(b + 1, mine, i)
        when_gateway(b, lambda: when_top(b, do), 0)

    def share_arrived(b, yes, i):
        def do():
            p = other(i)
            share(b, p).wait_recv()
            add_up(b, p)
            begin(b + 1, other, i)
        when_gateway(b, lambda: when_top(b, do), yes)

    def when_outer(yes, do):
        pl.when(outer == yes)(do)

    def outer_pair(m):
        def do():
            for i in (2 * m, 2 * m + 1):
                cross(core, mine(i)).wait_recv()
            add_up(core, mine(by_core(m)))
            begin_far(core + 1, m)
        when_outer(1, do)

    def core_pair(m):
        def do():
            for i in (2 * m, 2 * m + 1):
                cross(core, mine(i)).wait_recv()
            add_up(core, mine(by_core(m)))

            @pl.when((1 - bit[top]) * bit[core] == 1)
            def _():
                for i in (2 * m, 2 * m + 1):
                    for n in range(1, len(targets)):
                        spread(mine(i), n, i).start()

            begin_far(core + 1, m)
        when_gateway(top, do)

    def low_arrived(side, yes, i):
        @pl.when((1 - bit[top]) * bit[core] == 1)
        def _():
            when_gateway(top, lambda: spread(side(i), 0, i).wait_recv(), yes)

    def core_arrived(side, yes, i):
        def do():
            when_high(core, lambda: cross(core, side(i)).wait_recv())
        when_gateway(top, lambda: when_top(top, do), yes)

    def passed_on(m):
        return m == half // 2 - 1

    def forward(b, p, n, m):
        where = rows_of(p)
        return pltpu.make_async_remote_copy(
            src_ref=buckets.at[b, where], dst_ref=buckets.at[b, where],
            send_sem=send_sem.at[(3 * b + 1) * heads + n * (half // 2) + m], recv_sem=recv_sem.at[3 * b * heads + p],
            device_id=peer(targets[n]), device_id_type=MESH_ID,
        )

    def each_aim(b, m, do):
        def one(n):
            do(far_copy(b, mine(by_core(m)), n, m))
        one(0)

        @pl.when(outer == 0)
        def _():
            for n in range(1, len(targets)):
                if n == 2:
                    if not passed_on(m):
                        pl.when(bit[top] == 0)(lambda: one(2))
                elif passed_on(m):
                    pl.when(bit[top] == 1)(lambda: one(n))
                else:
                    one(n)

    def each_forward(b, m, do):
        if passed_on(m):
            @pl.when((1 - bit[top]) * gateway(top) == 1)
            def _():
                for n in range(1, len(targets)):
                    do(forward(b, mine(by_core(m)), n, m))

    def landing(side, kind, m):
        if side is mine:
            if kind == 0:
                return gateway(top) == 1 if passed_on(m) else outer == 0
            return outer == 1 if kind == 1 else (1 - gateway(top)) * (1 - bit[top]) == 1
        if kind == 0:
            return bit[top] == 1 if passed_on(m) else bit[top] >= 0
        return bit[top] == 0

    def begin_far(b, m):
        if b < bits:
            when_low(b, lambda: each_aim(b, m, lambda c: c.start()))

    def far_arrived(b, side, kind, m):
        p = side(by_core(m))

        def take():
            far_copy(b, p, 0, 0).wait_recv()
            share(b, p).start()
            if side is mine and kind == 0:
                each_forward(b, m, lambda c: c.start())

        def do():
            when_high(b, take)
            if side is mine and kind < 2 and b < bits - 1:
                @pl.when(gateway(top) + kind > 0)
                def _():
                    add_up(b, p)
                    begin_far(b + 1, m)
        pl.when(landing(side, kind, m))(do)

    def far_share_arrived(b, side, kind, m):
        def do():
            when_high(b, lambda: share(b, side(by_core(m, True))).wait_recv())
        pl.when(landing(side, kind, m))(do)

    when = {}
    for n, (side, i) in enumerate([(mine, i) for i in range(half)] + [(other, i) for i in range(half)]):
        when[side, i] = flight(0, STATE_TIME * (n + 1), STEP, LATENCY)
    for b in range(2):
        later = {}
        for (side, i), at in sorted(when.items(), key=lambda e: e[1]):
            if held_back(b, side, i):
                event(at, arrived, b, side, i, 0)
            else:
                event(at, arrived, b, side, i)
            later[side, i] = flight(1, at, STEP, LATENCY)
        if b == 0:
            when = later
    whole_at = dict(when)
    early = {}
    for b in range(2, core):
        later = {}
        for i in range(half):
            at = flight(("gate", b), when[mine, i], STEP, LATENCY)
            event(at, cross_arrived, b, i)
            early[i] = at
            near_share = max(flight(("share", b), at, STEP, LATENCY), when[other, i] + 0.01)
            event(near_share, share_arrived, b, 1, i)
            relayed = max(flight(("relay", b), at, STEP, LATENCY), when[mine, i] + 0.01)
            event(relayed, relay_arrived, b, i)
            last = max(flight(("last", b), relayed, STEP, LATENCY), when[other, i] + 0.01)
            if b == top and held_back(1, other, i):
                event(relayed + STEP, arrived, 1, other, i, 1)
                whole_at[other, i] = max(whole_at[other, i], relayed + STEP)
                last = max(last, relayed + STEP + 0.02)
            event(last, share_arrived, b, 0, i)
            later[mine, i] = relayed
            later[other, i] = last
            if b == core - 1:
                event(near_share + CORE_LATENCY, core_arrived, other, 1, i)
                if i % 2 == 1:
                    event(relayed + CORE_LATENCY, outer_pair, i // 2)
                event(last + CORE_LATENCY, core_arrived, other, 0, i)
        when = later
    done = {i: max(when[mine, i], when[other, i]) + CORE_LATENCY for i in range(half)}
    for m in range(half // 2):
        at = early[2 * m + 1] + CORE_LATENCY
        event(at, core_pair, m)
        for i in (2 * m, 2 * m + 1):
            landed = flight("low", at, STEP, LATENCY + 0.5)
            event(landed, low_arrived, other, 1, i)
            event(landed, low_arrived, mine, 0, i)
            event(landed + 0.5, low_arrived, other, 0, i)
        outer_at = when[mine, 2 * m + 1] + CORE_LATENCY
        for b in range(core + 1, bits):
            for side in (mine, other):
                landed = flight(b, at, STEP, LATENCY + 0.7)
                event(landed, far_arrived, b, side, 0, m)
                event(landed + CORE_LATENCY, far_share_arrived, b, side, 0, m)
            passed = landed
            if passed_on(m):
                passed = flight(("forward", b), landed, STEP, LATENCY + 0.4)
                for side in (mine, other):
                    event(passed, far_arrived, b, side, 2, m)
                    event(passed + CORE_LATENCY, far_share_arrived, b, side, 2, m)
            outer_at = flight(("outer", b), outer_at, STEP, LATENCY)
            event(outer_at, far_arrived, b, mine, 1, m)
            event(outer_at + CORE_LATENCY, far_share_arrived, b, mine, 1, m)
            at = landed
            landed = max(landed, outer_at, passed)
            for i in (2 * m, 2 * m + 1):
                done[i] = max(done[i], landed + CORE_LATENCY)

    def far_head(h, chosen, last):
        where = pl.ds(pl.multiple_of(h * width, width), width)
        high = []
        low = []
        for b in chosen:
            whole = jnp.where(bit[b] == 1, buckets[b, where, :], 0.0)
            top = whole.astype(jnp.bfloat16)
            high.append(top)
            low.append((whole - top.astype(jnp.float32)).astype(jnp.bfloat16))
        both = jnp.concatenate([jnp.concatenate(high, 0), jnp.concatenate(low, 0)], 1)
        for ti in range(length // TILE):
            cols = pl.ds(ti * TILE, TILE)
            query = q_heads[h, cols, :]
            products = nt_dot(both, jnp.concatenate([query, query], 1))
            total = near[h, :, cols]
            for n, b in enumerate(chosen):
                total = total + products[n * width : (n + 1) * width] * w_in[h, pl.ds(local_bits + 1 + b, 1), cols]
            if last:
                scale = lax.rsqrt(jnp.mean(total * total, 0, keepdims=True) + EPSILON)
                wide_b[pl.ds(ti * TILE * heads + h, TILE, stride=heads), :] = (total * scale).T
            else:
                near[h, :, cols] = total

    first = [0, 1]
    last = list(range(2, bits))
    loops = [
        (heads, NEAR_TIME, [0] * heads, lambda i: near_head(i)),
        (
            half // 2, 0.66, [whole_at[mine, 2 * i + 1] for i in range(half // 2)],
            lambda i: (far_head(mine(2 * i), first, False), far_head(mine(2 * i + 1), first, False)),
        ),
        (
            half // 2, 0.66, [whole_at[other, 2 * i + 1] for i in range(half // 2)],
            lambda i: (far_head(other(2 * i), first, False), far_head(other(2 * i + 1), first, False)),
        ),
        (half, 0.7, [done[i] for i in range(half)], lambda i: (far_head(mine(i), last, True), far_head(other(i), last, True))),
    ]
    waiting = sorted(events, key=lambda e: e[0])
    clock = STATE_TIME * heads
    for count, cost, needs, work in loops:
        slots = []
        for need in needs:
            slots.append([])
            while waiting and waiting[0][0] <= max(clock, need + 0.02):
                at, do = waiting.pop(0)
                slots[-1].append(do)
                clock = max(clock, at)
            clock += cost

        def one(i, _, slots=slots, work=work):
            for at, group in enumerate(slots):
                def run(group=group):
                    for do in group:
                        do()
                if group:
                    pl.when(i == at)(run)
            work(i)
            return 0

        lax.fori_loop(0, count, one, 0)
    assert not waiting

    def sent(i, _):
        for side in (mine, other):
            p = side(i)
            cross(0, p).wait_send()
            when_lean(1, sends_1, lambda: cross(1, p).wait_send())
            amount = (1 - bit[core]) * bit[top]
            if side is mine:
                amount = gateway(top) + bit[top]

            @pl.when(amount > 0)
            def _():
                cross(core, p).wait_send()
        for b in range(2, core):
            when_top(b, lambda: share(b, mine(i)).wait_send())

            def do():
                cross(b, mine(i)).wait_send()
                when_top(b, lambda: relay(b, mine(i)).wait_send())
            when_gateway(b, do)

        @pl.when((1 - bit[top]) * bit[core] * gateway(top) == 1)
        def _():
            for n in range(1, len(targets)):
                spread(mine(i), n, i).wait_send()
        return 0

    lax.fori_loop(0, half, sent, 0)

    def far_sent(m):
        for b in range(core + 1, bits):
            def done_far():
                when_low(b, lambda: each_aim(b, m, lambda c: c.wait_send()))
            pl.when(gateway(top) + bit[top] > 0)(done_far)

            def do_share():
                each_forward(b, m, lambda c: c.wait_send())
                for side in (mine, other):
                    share(b, side(by_core(m))).wait_send()
            when_high(b, do_share)

    for m in range(half // 2):
        far_sent(m)


def per_device(query, key, value, level_weight):
    length, heads, width = query.shape
    short_bits = log2(lax.axis_size("short"))
    long_bits = log2(lax.axis_size("long"))
    bits = short_bits + long_bits
    rows = heads * width
    copies = 3 * bits * heads + 2 * heads
    level_weight = jnp.transpose(level_weight, (1, 0, 2))
    total = pl.pallas_call(
        functools.partial(kernel, short_bits, long_bits, heads, length, width),
        out_shape=pltpu.VMEM((length * heads, width), jnp.float32),
        in_specs=[pl.BlockSpec(memory_space=pl.ANY)] * 4,
        out_specs=pl.BlockSpec(memory_space=pltpu.VMEM),
        scratch_shapes=[
            pltpu.VMEM(query.shape, jnp.bfloat16),
            pltpu.VMEM(query.shape, jnp.bfloat16),
            pltpu.VMEM(query.shape, jnp.bfloat16),
            pltpu.VMEM((heads, level_weight.shape[0], length), jnp.float32),
            pltpu.VMEM((length * heads, width), jnp.float32),
            pltpu.VMEM((heads, length, width), jnp.bfloat16),
            pltpu.VMEM((heads, length, width), jnp.bfloat16),
            pltpu.VMEM((heads, width, length), jnp.bfloat16),
            pltpu.VMEM((heads, width, length), jnp.float32),
            pltpu.VMEM((SUB, SUB), jnp.int32),
            pltpu.VMEM((bits, rows, width), jnp.float32),
            pltpu.VMEM((bits, rows, width), jnp.float32),
            pltpu.SemaphoreType.DMA((copies,)),
            pltpu.SemaphoreType.DMA((copies,)),
            pltpu.SemaphoreType.DMA((2 * CHUNKS + 1 + heads,)),
        ],
        compiler_params=pltpu.CompilerParams(
            collective_id=0, has_side_effects=True, vmem_limit_bytes=52 * 1024 * 1024
        ),
    )(query, key, value, level_weight)
    return total.reshape(query.shape).astype(jnp.bfloat16)


def solution(mesh):
    rows = P(("long", "short"), None)
    return jax.shard_map(
        per_device,
        mesh=mesh,
        in_specs=(rows, rows, rows, P(None, None, ("long", "short"))),
        out_specs=rows,
        check_vma=False,
    )
```

```python
import functools

import jax
import jax.numpy as jnp
from jax import lax
from jax.experimental import pallas as pl
from jax.experimental.pallas import tpu as pltpu
from jax.sharding import PartitionSpec as P

EPSILON = 1e-06
TILE = 256
NEAR_TILE = 512
SUB = 128
STATE_TIME = 0.43
NEAR_TIME = 0.95
STEP = 1.31
LATENCY = 2.2
CORE_LATENCY = 1.0
CHUNKS = 4
MESH_ID = pl.DeviceIdType.MESH


def log2(n):
    return n.bit_length() - 1


def subsets(bits):
    found = [tuple(b for i, b in enumerate(bits) if mask >> i & 1) for mask in range(1 << len(bits))]
    return sorted(found, key=len)


def nt_dot(a, b):
    return lax.dot_general(a, b, (((1,), (1,)), ((), ())), preferred_element_type=jnp.float32)


def kernel(
    short_bits, long_bits, heads, length, width,
    q_ref, k_ref, v_ref, w_ref, wide_b,
    k_in, v_in, q_in, w_in, wide_a, q_heads, k_heads, v_turned, near, levels, sums, buckets, send_sem, recv_sem, load_sem,
):
    bits = short_bits + long_bits
    rows = heads * width
    local_bits = log2(length)
    short_pos = lax.axis_index("short")
    long_pos = lax.axis_index("long")
    bit = [(short_pos // (1 << b)) % 2 for b in range(short_bits)]
    bit += [(long_pos // (1 << b)) % 2 for b in range(long_bits)]

    core = short_bits
    half = heads // 2
    targets = subsets([0, core - 2])

    def gateway(b):
        return bit[b - 1] + bit[b] - 2 * bit[b - 1] * bit[b]

    def peer(flips):
        short = short_pos
        long = long_pos
        for b in flips:
            if b < short_bits:
                short = short + (1 - 2 * bit[b]) * (1 << b)
            else:
                long = long + (1 - 2 * bit[b]) * (1 << b - short_bits)
        return {"short": short, "long": long}

    def mine(i):
        return bit[0] * half + i

    def other(i):
        return (1 - bit[0]) * half + i

    def rows_of(p):
        return pl.ds(pl.multiple_of(p * width, width), width)

    def copy(src, dst, b, p, bank, sent, to):
        where = rows_of(p)
        base = (3 * b + bank) * heads
        return pltpu.make_async_remote_copy(
            src_ref=src.at[b, where], dst_ref=dst.at[b, where],
            send_sem=send_sem.at[base + sent], recv_sem=recv_sem.at[base + p],
            device_id=peer(to), device_id_type=MESH_ID,
        )

    def cross(b, p):
        return copy(sums, buckets, b, p, 0, p, (b,) if b < 2 or b >= core else (b - 1, b))

    def relay(b, p):
        return copy(buckets, buckets, b, p, 1, p, (b - 1,))

    def share(b, p):
        return copy(buckets, buckets, b, p, 2, p, (0,) if b < core else (core,))

    top = core - 1
    lean = core - 2 == 1
    sends_1 = bit[top] + 1 - bit[1]
    takes_1 = bit[top] + bit[1]

    def spread(p, n, i):
        where = rows_of(p)
        base = 3 * bits * heads
        return pltpu.make_async_remote_copy(
            src_ref=buckets.at[core, where], dst_ref=buckets.at[core, where],
            send_sem=send_sem.at[base + n * half + i], recv_sem=recv_sem.at[base + p],
            device_id=peer(targets[n]), device_id_type=MESH_ID,
        )

    def when_lean(b, amount, do):
        if b == 1 and lean:
            pl.when(amount > 0)(do)
        else:
            do()

    def when_top(b, do):
        if b == top:
            pl.when(bit[top] == 1)(do)
        else:
            do()

    def far_copy(b, p, n, m):
        return copy(sums, buckets, b, p, 0, n * (half // 2) + m, (b,) + targets[n])

    peers = [(b,) for b in (0, 1)] + [(b,) for b in range(1, core - 1) if b > 1] + [(b - 1, b) for b in range(2, core)]
    peers += [(0, core - 2), (core,)] + [(b,) + c for b in range(core + 1, bits) for c in targets]

    barrier = pltpu.get_barrier_semaphore()
    for flips in peers:
        pl.semaphore_signal(barrier, inc=1, device_id=peer(flips), device_id_type=MESH_ID)

    chunk = length // CHUNKS
    first_loads = []
    for c in range(CHUNKS):
        for n, (src, dst) in enumerate([(k_ref, k_in), (v_ref, v_in)]):
            at = pl.ds(c * chunk, chunk)
            first_loads.append(pltpu.make_async_copy(src.at[at], dst.at[at], load_sem.at[2 * c + n]))
    loads = [pltpu.make_async_copy(q_ref, q_in, load_sem.at[2 * CHUNKS])]
    for h in range(heads):
        loads.append(pltpu.make_async_copy(w_ref.at[:, h, :], w_in.at[h], load_sem.at[2 * CHUNKS + 1 + h]))
    for load in first_loads:
        load.start()

    part = 64

    def widen(src, dst, start, stop):
        def step(i, _):
            at = pl.multiple_of(i * part, part)
            x = src[pl.ds(at, part)].astype(jnp.float32)
            dst[pl.ds(pl.multiple_of(at * heads, part * heads), part * heads), :] = x.reshape(part * heads, width)
            return 0
        lax.fori_loop(start // part, stop // part, step, 0)

    for c in range(CHUNKS):
        for n, (src, dst) in enumerate([(k_in, wide_a), (v_in, wide_b)]):
            first_loads[2 * c + n].wait()
            if c == CHUNKS - 1 and n == 1:
                for load in loads:
                    load.start()
            widen(src, dst, c * chunk, (c + 1) * chunk)

    def state_step(i, _):
        h = (1 - bit[0] + i // half * (2 * bit[0] - 1)) * half + i % half
        key = wide_a[pl.ds(h, length, stride=heads), :].astype(jnp.bfloat16)
        turned = wide_b[pl.ds(h, length, stride=heads), :].T.astype(jnp.bfloat16)
        k_heads[h] = key
        v_turned[h] = turned
        sums[0, pl.ds(pl.multiple_of(h * width, width), width), :] = jnp.dot(turned, key, preferred_element_type=jnp.float32)

        @pl.when(i == 0)
        def _():
            pl.semaphore_wait(barrier, len(peers))

        cross(0, h).start()
        return 0

    lax.fori_loop(0, heads, state_step, 0)

    row = lax.broadcasted_iota(jnp.int32, (SUB, SUB), 0)
    col = lax.broadcasted_iota(jnp.int32, (SUB, SUB), 1)
    differ = jnp.bitwise_xor(row, col)
    table = jnp.zeros((SUB, SUB), jnp.int32)
    for b in range(log2(SUB)):
        table = table + (differ >= 1 << b).astype(jnp.int32)
    levels[...] = jnp.where(row <= col, table, -1)

    loads[0].wait()
    widen(q_in, wide_a, 0, length)
    for load in loads[1:]:
        load.wait()

    def near_head(h):
        q_heads[h] = wide_a[pl.ds(h, length, stride=heads), :].astype(jnp.bfloat16)
        level = levels[...]
        for ti in range(length // NEAR_TILE):
            cols = pl.ds(ti * NEAR_TILE, NEAR_TILE)
            query = q_heads[h, cols, :]
            pieces = []
            for si in range(ti + 1):
                scores = nt_dot(k_heads[h, pl.ds(si * NEAR_TILE, NEAR_TILE), :], query)
                if si < ti:
                    weighted = scores * w_in[h, pl.ds(log2(NEAR_TILE) + (ti ^ si).bit_length(), 1), cols]
                else:
                    columns = []
                    for a in range(NEAR_TILE // SUB):
                        at = pl.ds(ti * NEAR_TILE + a * SUB, SUB)
                        parts = []
                        for c in range(NEAR_TILE // SUB):
                            block = scores[c * SUB : (c + 1) * SUB, a * SUB : (a + 1) * SUB]
                            if c < a:
                                parts.append(block * w_in[h, pl.ds(log2(SUB) + (a ^ c).bit_length(), 1), at])
                            elif c > a:
                                parts.append(jnp.zeros_like(block))
                            else:
                                mixing = jnp.zeros((SUB, SUB), jnp.float32)
                                for n in range(log2(SUB) + 1):
                                    mixing = jnp.where(level == n, w_in[h, pl.ds(n, 1), at], mixing)
                                parts.append(mixing * block)
                        columns.append(jnp.concatenate(parts, 0))
                    weighted = jnp.concatenate(columns, 1)
                pieces.append(weighted.astype(jnp.bfloat16))
            near[h, :, cols] = jnp.dot(
                v_turned[h, :, pl.ds(0, (ti + 1) * NEAR_TILE)], jnp.concatenate(pieces, 0),
                preferred_element_type=jnp.float32,
            )

    def add_up(b, p):
        if b < bits - 1:
            where = rows_of(p)
            sums[b + 1, where, :] = sums[b, where, :] + buckets[b, where, :]

    def when_low(b, do):
        if b < bits - 1 and b != core:
            do()
        else:
            pl.when(bit[b] == 0)(do)

    def when_high(b, do):
        if b < bits - 1 and b != core:
            do()
        else:
            pl.when(bit[b] == 1)(do)

    def when_gateway(b, do, yes=1):
        pl.when(gateway(b) == yes)(do)

    def by_core(m, away=False):
        return 2 * m + (1 - bit[core] if away else bit[core])

    events = []
    free = {}

    def flight(link, ready, step, latency):
        end = max(free.get(link, 0), ready) + step
        free[link] = end
        return end + latency

    def event(at, do, *given):
        events.append((at, functools.partial(do, *given)))

    outer = (1 - gateway(top)) * bit[top]

    def held_back(b, side, i):
        return lean and b == 1 and side is other and i >= half // 2

    def begin(b, side, i):
        p = side(i)
        if b < 2:
            go = sends_1
            if held_back(b, side, i):
                go = go * (1 - bit[top] * gateway(top))
            when_lean(b, go, lambda: cross(b, p).start())
        elif b < core:
            if side is mine:
                when_gateway(b, lambda: cross(b, p).start())
        elif b == core:
            if side is mine:
                cross(b, p).start()
            else:
                when_low(b, lambda: cross(b, p).start())

    def arrived(b, side, i, kind=None):
        def do():
            p = side(i)
            cross(b, p).wait_recv()
            add_up(b, p)
            begin(b + 1, side, i)
        if kind is None:
            when_lean(b, takes_1, do)
        else:
            pl.when(takes_1 * (1 - outer if kind == 0 else outer) > 0)(do)

    def cross_arrived(b, i):
        def do():
            p = mine(i)
            cross(b, p).wait_recv()

            def on():
                relay(b, p).start()
                share(b, p).start()
                if b == top and held_back(1, other, i):
                    cross(1, other(i)).start()
            when_top(b, on)
            add_up(b, p)
            begin(b + 1, mine, i)
        when_gateway(b, do)

    def relay_arrived(b, i):
        def do():
            p = mine(i)
            relay(b, p).wait_recv()
            share(b, p).start()
            add_up(b, p)
            begin(b + 1, mine, i)
        when_gateway(b, lambda: when_top(b, do), 0)

    def share_arrived(b, yes, i):
        def do():
            p = other(i)
            share(b, p).wait_recv()
            add_up(b, p)
            begin(b + 1, other, i)
        when_gateway(b, lambda: when_top(b, do), yes)

    def when_outer(yes, do):
        pl.when(outer == yes)(do)

    def outer_pair(m):
        def do():
            for i in (2 * m, 2 * m + 1):
                cross(core, mine(i)).wait_recv()
            add_up(core, mine(by_core(m)))
            begin_far(core + 1, m)
        when_outer(1, do)

    def core_pair(m):
        def do():
            for i in (2 * m, 2 * m + 1):
                cross(core, mine(i)).wait_recv()
            add_up(core, mine(by_core(m)))

            @pl.when((1 - bit[top]) * bit[core] == 1)
            def _():
                for i in (2 * m, 2 * m + 1):
                    for n in range(1, len(targets)):
                        spread(mine(i), n, i).start()

            begin_far(core + 1, m)
        when_gateway(top, do)

    def low_arrived(side, yes, i):
        @pl.when((1 - bit[top]) * bit[core] == 1)
        def _():
            when_gateway(top, lambda: spread(side(i), 0, i).wait_recv(), yes)

    def core_arrived(side, yes, i):
        def do():
            when_high(core, lambda: cross(core, side(i)).wait_recv())
        when_gateway(top, lambda: when_top(top, do), yes)

    def passed_on(m):
        return m == half // 2 - 1

    def forward(b, p, n, m):
        where = rows_of(p)
        return pltpu.make_async_remote_copy(
            src_ref=buckets.at[b, where], dst_ref=buckets.at[b, where],
            send_sem=send_sem.at[(3 * b + 1) * heads + n * (half // 2) + m], recv_sem=recv_sem.at[3 * b * heads + p],
            device_id=peer(targets[n]), device_id_type=MESH_ID,
        )

    def each_aim(b, m, do):
        def one(n):
            do(far_copy(b, mine(by_core(m)), n, m))
        one(0)

        @pl.when(outer == 0)
        def _():
            for n in range(1, len(targets)):
                if n == 2:
                    if not passed_on(m):
                        pl.when(bit[top] == 0)(lambda: one(2))
                elif passed_on(m):
                    pl.when(bit[top] == 1)(lambda: one(n))
                else:
                    one(n)

    def each_forward(b, m, do):
        if passed_on(m):
            @pl.when((1 - bit[top]) * gateway(top) == 1)
            def _():
                for n in range(1, len(targets)):
                    do(forward(b, mine(by_core(m)), n, m))

    def landing(side, kind, m):
        if side is mine:
            if kind == 0:
                return gateway(top) == 1 if passed_on(m) else outer == 0
            return outer == 1 if kind == 1 else (1 - gateway(top)) * (1 - bit[top]) == 1
        if kind == 0:
            return bit[top] == 1 if passed_on(m) else bit[top] >= 0
        return bit[top] == 0

    def begin_far(b, m):
        if b < bits:
            when_low(b, lambda: each_aim(b, m, lambda c: c.start()))

    def far_arrived(b, side, kind, m):
        p = side(by_core(m))

        def take():
            far_copy(b, p, 0, 0).wait_recv()
            share(b, p).start()
            if side is mine and kind == 0:
                each_forward(b, m, lambda c: c.start())

        def do():
            when_high(b, take)
            if side is mine and kind < 2 and b < bits - 1:
                @pl.when(gateway(top) + kind > 0)
                def _():
                    add_up(b, p)
                    begin_far(b + 1, m)
        pl.when(landing(side, kind, m))(do)

    def far_share_arrived(b, side, kind, m):
        def do():
            when_high(b, lambda: share(b, side(by_core(m, True))).wait_recv())
        pl.when(landing(side, kind, m))(do)

    when = {}
    for n, (side, i) in enumerate([(mine, i) for i in range(half)] + [(other, i) for i in range(half)]):
        when[side, i] = flight(0, STATE_TIME * (n + 1), STEP, LATENCY)
    for b in range(2):
        later = {}
        for (side, i), at in sorted(when.items(), key=lambda e: e[1]):
            if held_back(b, side, i):
                event(at, arrived, b, side, i, 0)
            else:
                event(at, arrived, b, side, i)
            later[side, i] = flight(1, at, STEP, LATENCY)
        if b == 0:
            when = later
    whole_at = dict(when)
    early = {}
    for b in range(2, core):
        later = {}
        for i in range(half):
            at = flight(("gate", b), when[mine, i], STEP, LATENCY)
            event(at, cross_arrived, b, i)
            early[i] = at
            near_share = max(flight(("share", b), at, STEP, LATENCY), when[other, i] + 0.01)
            event(near_share, share_arrived, b, 1, i)
            relayed = max(flight(("relay", b), at, STEP, LATENCY), when[mine, i] + 0.01)
            event(relayed, relay_arrived, b, i)
            last = max(flight(("last", b), relayed, STEP, LATENCY), when[other, i] + 0.01)
            if b == top and held_back(1, other, i):
                event(relayed + STEP, arrived, 1, other, i, 1)
                whole_at[other, i] = max(whole_at[other, i], relayed + STEP)
                last = max(last, relayed + STEP + 0.02)
            event(last, share_arrived, b, 0, i)
            later[mine, i] = relayed
            later[other, i] = last
            if b == core - 1:
                event(near_share + CORE_LATENCY, core_arrived, other, 1, i)
                if i % 2 == 1:
                    event(relayed + CORE_LATENCY, outer_pair, i // 2)
                event(last + CORE_LATENCY, core_arrived, other, 0, i)
        when = later
    done = {i: max(when[mine, i], when[other, i]) + CORE_LATENCY for i in range(half)}
    for m in range(half // 2):
        at = early[2 * m + 1] + CORE_LATENCY
        event(at, core_pair, m)
        for i in (2 * m, 2 * m + 1):
            landed = flight("low", at, STEP, LATENCY + 0.5)
            event(landed, low_arrived, other, 1, i)
            event(landed, low_arrived, mine, 0, i)
            event(landed + 0.5, low_arrived, other, 0, i)
        outer_at = when[mine, 2 * m + 1] + CORE_LATENCY
        for b in range(core + 1, bits):
            for side in (mine, other):
                landed = flight(b, at, STEP, LATENCY + 0.7)
                event(landed, far_arrived, b, side, 0, m)
                event(landed + CORE_LATENCY, far_share_arrived, b, side, 0, m)
            passed = landed
            if passed_on(m):
                passed = flight(("forward", b), landed, STEP, LATENCY + 0.4)
                for side in (mine, other):
                    event(passed, far_arrived, b, side, 2, m)
                    event(passed + CORE_LATENCY, far_share_arrived, b, side, 2, m)
            outer_at = flight(("outer", b), outer_at, STEP, LATENCY)
            event(outer_at, far_arrived, b, mine, 1, m)
            event(outer_at + CORE_LATENCY, far_share_arrived, b, mine, 1, m)
            at = landed
            landed = max(landed, outer_at, passed)
            for i in (2 * m, 2 * m + 1):
                done[i] = max(done[i], landed + CORE_LATENCY)

    def far_head(h, chosen, last):
        where = pl.ds(pl.multiple_of(h * width, width), width)
        high = []
        low = []
        for b in chosen:
            whole = jnp.where(bit[b] == 1, buckets[b, where, :], 0.0)
            top = whole.astype(jnp.bfloat16)
            high.append(top)
            low.append((whole - top.astype(jnp.float32)).astype(jnp.bfloat16))
        both = jnp.concatenate([jnp.concatenate(high, 0), jnp.concatenate(low, 0)], 1)
        for ti in range(length // TILE):
            cols = pl.ds(ti * TILE, TILE)
            query = q_heads[h, cols, :]
            products = nt_dot(both, jnp.concatenate([query, query], 1))
            total = near[h, :, cols]
            for n, b in enumerate(chosen):
                total = total + products[n * width : (n + 1) * width] * w_in[h, pl.ds(local_bits + 1 + b, 1), cols]
            if last:
                scale = lax.rsqrt(jnp.mean(total * total, 0, keepdims=True) + EPSILON)
                wide_b[pl.ds(ti * TILE * heads + h, TILE, stride=heads), :] = (total * scale).T
            else:
                near[h, :, cols] = total

    first = [0, 1]
    last = list(range(2, bits))
    final = [max(done[2 * m], done[2 * m + 1]) for m in range(half // 2)]

    def sent_early(i, _):
        for side in (mine, other):
            p = side(i)
            cross(0, p).wait_send()
            when_lean(1, sends_1, lambda: cross(1, p).wait_send())
        for b in range(2, core):
            when_gateway(b, lambda: cross(b, mine(i)).wait_send())
        return 0

    loops = [
        (heads, NEAR_TIME, [0] * heads, lambda i: near_head(i)),
        (
            half // 2, 0.66, [whole_at[mine, 2 * i + 1] for i in range(half // 2)],
            lambda i: (far_head(mine(2 * i), first, False), far_head(mine(2 * i + 1), first, False)),
        ),
        (
            half // 2, 0.66, [whole_at[other, 2 * i + 1] for i in range(half // 2)],
            lambda i: (far_head(other(2 * i), first, False), far_head(other(2 * i + 1), first, False)),
        ),
        (half // 2, 1.3, final, lambda i: [far_head(side(2 * i + n), last, True) for side in (mine, other) for n in range(2)]),
    ]
    waiting = sorted(events, key=lambda e: e[0])
    clock = STATE_TIME * heads
    for count, cost, needs, work in loops:
        slots = []
        for need in needs:
            slots.append([])
            while waiting and waiting[0][0] <= max(clock, need + 0.02):
                at, do = waiting.pop(0)
                slots[-1].append(do)
                clock = max(clock, at)
            clock += cost

        def one(i, _, slots=slots, work=work):
            for at, group in enumerate(slots):
                def run(group=group):
                    for do in group:
                        do()
                if group:
                    pl.when(i == at)(run)
            work(i)
            return 0

        if needs is final:
            lax.fori_loop(0, half, sent_early, 0)
        lax.fori_loop(0, count, one, 0)
    assert not waiting

    def sent(i, _):
        for side in (mine, other):
            p = side(i)
            amount = (1 - bit[core]) * bit[top]
            if side is mine:
                amount = gateway(top) + bit[top]

            @pl.when(amount > 0)
            def _():
                cross(core, p).wait_send()
        for b in range(2, core):
            when_top(b, lambda: share(b, mine(i)).wait_send())

            def do():
                when_top(b, lambda: relay(b, mine(i)).wait_send())
            when_gateway(b, do)

        @pl.when((1 - bit[top]) * bit[core] * gateway(top) == 1)
        def _():
            for n in range(1, len(targets)):
                spread(mine(i), n, i).wait_send()
        return 0

    lax.fori_loop(0, half, sent, 0)

    def far_sent(m):
        for b in range(core + 1, bits):
            def done_far():
                when_low(b, lambda: each_aim(b, m, lambda c: c.wait_send()))
            pl.when(gateway(top) + bit[top] > 0)(done_far)

            def do_share():
                each_forward(b, m, lambda c: c.wait_send())
                for side in (mine, other):
                    share(b, side(by_core(m))).wait_send()
            when_high(b, do_share)

    for m in range(half // 2):
        far_sent(m)


def per_device(query, key, value, level_weight):
    length, heads, width = query.shape
    short_bits = log2(lax.axis_size("short"))
    long_bits = log2(lax.axis_size("long"))
    bits = short_bits + long_bits
    rows = heads * width
    copies = 3 * bits * heads + 2 * heads
    level_weight = jnp.transpose(level_weight, (1, 0, 2))
    total = pl.pallas_call(
        functools.partial(kernel, short_bits, long_bits, heads, length, width),
        out_shape=pltpu.VMEM((length * heads, width), jnp.float32),
        in_specs=[pl.BlockSpec(memory_space=pl.ANY)] * 4,
        out_specs=pl.BlockSpec(memory_space=pltpu.VMEM),
        scratch_shapes=[
            pltpu.VMEM(query.shape, jnp.bfloat16),
            pltpu.VMEM(query.shape, jnp.bfloat16),
            pltpu.VMEM(query.shape, jnp.bfloat16),
            pltpu.VMEM((heads, level_weight.shape[0], length), jnp.float32),
            pltpu.VMEM((length * heads, width), jnp.float32),
            pltpu.VMEM((heads, length, width), jnp.bfloat16),
            pltpu.VMEM((heads, length, width), jnp.bfloat16),
            pltpu.VMEM((heads, width, length), jnp.bfloat16),
            pltpu.VMEM((heads, width, length), jnp.float32),
            pltpu.VMEM((SUB, SUB), jnp.int32),
            pltpu.VMEM((bits, rows, width), jnp.float32),
            pltpu.VMEM((bits, rows, width), jnp.float32),
            pltpu.SemaphoreType.DMA((copies,)),
            pltpu.SemaphoreType.DMA((copies,)),
            pltpu.SemaphoreType.DMA((2 * CHUNKS + 1 + heads,)),
        ],
        compiler_params=pltpu.CompilerParams(
            collective_id=0, has_side_effects=True, vmem_limit_bytes=52 * 1024 * 1024
        ),
    )(query, key, value, level_weight)
    return total.reshape(query.shape).astype(jnp.bfloat16)


def solution(mesh):
    rows = P(("long", "short"), None)
    return jax.shard_map(
        per_device,
        mesh=mesh,
        in_specs=(rows, rows, rows, P(None, None, ("long", "short"))),
        out_specs=rows,
        check_vma=False,
    )
```

```python
import functools

import jax
import jax.numpy as jnp
from jax import lax
from jax.experimental import pallas as pl
from jax.experimental.pallas import tpu as pltpu
from jax.sharding import PartitionSpec as P

EPSILON = 1e-06
TILE = 256
NEAR_TILE = 512
SUB = 128
STATE_TIME = 0.43
NEAR_TIME = 0.95
STEP = 1.31
LATENCY = 2.2
CORE_LATENCY = 1.0
CHUNKS = 4
MESH_ID = pl.DeviceIdType.MESH


def log2(n):
    return n.bit_length() - 1


def subsets(bits):
    found = [tuple(b for i, b in enumerate(bits) if mask >> i & 1) for mask in range(1 << len(bits))]
    return sorted(found, key=len)


def nt_dot(a, b):
    return lax.dot_general(a, b, (((1,), (1,)), ((), ())), preferred_element_type=jnp.float32)


def kernel(
    short_bits, long_bits, heads, length, width,
    q_ref, k_ref, v_ref, w_ref, wide_b,
    k_in, v_in, q_in, w_in, wide_a, q_heads, k_heads, v_turned, near, levels, sums, buckets, send_sem, recv_sem, load_sem,
):
    bits = short_bits + long_bits
    rows = heads * width
    local_bits = log2(length)
    short_pos = lax.axis_index("short")
    long_pos = lax.axis_index("long")
    bit = [(short_pos // (1 << b)) % 2 for b in range(short_bits)]
    bit += [(long_pos // (1 << b)) % 2 for b in range(long_bits)]

    core = short_bits
    half = heads // 2
    targets = subsets([0, core - 2])

    def gateway(b):
        return bit[b - 1] + bit[b] - 2 * bit[b - 1] * bit[b]

    def peer(flips):
        short = short_pos
        long = long_pos
        for b in flips:
            if b < short_bits:
                short = short + (1 - 2 * bit[b]) * (1 << b)
            else:
                long = long + (1 - 2 * bit[b]) * (1 << b - short_bits)
        return {"short": short, "long": long}

    def mine(i):
        return bit[0] * half + i

    def other(i):
        return (1 - bit[0]) * half + i

    def rows_of(p):
        return pl.ds(pl.multiple_of(p * width, width), width)

    def copy(src, dst, b, p, bank, sent, to):
        where = rows_of(p)
        base = (3 * b + bank) * heads
        return pltpu.make_async_remote_copy(
            src_ref=src.at[b, where], dst_ref=dst.at[b, where],
            send_sem=send_sem.at[base + sent], recv_sem=recv_sem.at[base + p],
            device_id=peer(to), device_id_type=MESH_ID,
        )

    def cross(b, p):
        return copy(sums, buckets, b, p, 0, p, (b,) if b < 2 or b >= core else (b - 1, b))

    def relay(b, p):
        return copy(buckets, buckets, b, p, 1, p, (b - 1,))

    def share(b, p):
        return copy(buckets, buckets, b, p, 2, p, (0,) if b < core else (core,))

    top = core - 1
    lean = core - 2 == 1
    sends_1 = bit[top] + 1 - bit[1]
    takes_1 = bit[top] + bit[1]

    def spread(p, n, i):
        where = rows_of(p)
        base = 3 * bits * heads
        return pltpu.make_async_remote_copy(
            src_ref=buckets.at[core, where], dst_ref=buckets.at[core, where],
            send_sem=send_sem.at[base + n * half + i], recv_sem=recv_sem.at[base + p],
            device_id=peer(targets[n]), device_id_type=MESH_ID,
        )

    def when_lean(b, amount, do):
        if b == 1 and lean:
            pl.when(amount > 0)(do)
        else:
            do()

    def when_top(b, do):
        if b == top:
            pl.when(bit[top] == 1)(do)
        else:
            do()

    def far_copy(b, p, n, m):
        return copy(sums, buckets, b, p, 0, n * (half // 2) + m, (b,) + targets[n])

    peers = [(b,) for b in (0, 1)] + [(b,) for b in range(1, core - 1) if b > 1] + [(b - 1, b) for b in range(2, core)]
    peers += [(0, core - 2), (core,)] + [(b,) + c for b in range(core + 1, bits) for c in targets]

    chunk = length // CHUNKS
    first_loads = []
    for c in range(CHUNKS):
        for n, (src, dst) in enumerate([(k_ref, k_in), (v_ref, v_in)]):
            at = pl.ds(c * chunk, chunk)
            first_loads.append(pltpu.make_async_copy(src.at[at], dst.at[at], load_sem.at[2 * c + n]))
    loads = [pltpu.make_async_copy(q_ref, q_in, load_sem.at[2 * CHUNKS])]
    for h in range(heads):
        loads.append(pltpu.make_async_copy(w_ref.at[:, h, :], w_in.at[h], load_sem.at[2 * CHUNKS + 1 + h]))
    for load in first_loads:
        load.start()

    barrier = pltpu.get_barrier_semaphore()
    for flips in peers:
        pl.semaphore_signal(barrier, inc=1, device_id=peer(flips), device_id_type=MESH_ID)

    part = 64

    def widen(src, dst, start, stop):
        def step(i, _):
            at = pl.multiple_of(i * part, part)
            x = src[pl.ds(at, part)].astype(jnp.float32)
            dst[pl.ds(pl.multiple_of(at * heads, part * heads), part * heads), :] = x.reshape(part * heads, width)
            return 0
        lax.fori_loop(start // part, stop // part, step, 0)

    for c in range(CHUNKS):
        for n, (src, dst) in enumerate([(k_in, wide_a), (v_in, wide_b)]):
            first_loads[2 * c + n].wait()
            if c == CHUNKS - 1 and n == 1:
                for load in loads:
                    load.start()
            widen(src, dst, c * chunk, (c + 1) * chunk)

    def state_of(i):
        h = (1 - bit[0] + i // half * (2 * bit[0] - 1)) * half + i % half
        key = wide_a[pl.ds(h, length, stride=heads), :].astype(jnp.bfloat16)
        turned = wide_b[pl.ds(h, length, stride=heads), :].T.astype(jnp.bfloat16)
        k_heads[h] = key
        v_turned[h] = turned
        sums[0, rows_of(h), :] = jnp.dot(turned, key, preferred_element_type=jnp.float32)
        return h

    def state_pair(n, _):
        first_two = [state_of(2 * n), state_of(2 * n + 1)]

        @pl.when(n == 0)
        def _():
            pl.semaphore_wait(barrier, len(peers))

        for h in first_two:
            cross(0, h).start()
        return 0

    lax.fori_loop(0, half, state_pair, 0)

    row = lax.broadcasted_iota(jnp.int32, (SUB, SUB), 0)
    col = lax.broadcasted_iota(jnp.int32, (SUB, SUB), 1)
    differ = jnp.bitwise_xor(row, col)
    table = jnp.zeros((SUB, SUB), jnp.int32)
    for b in range(log2(SUB)):
        table = table + (differ >= 1 << b).astype(jnp.int32)
    levels[...] = jnp.where(row <= col, table, -1)

    loads[0].wait()
    widen(q_in, wide_a, 0, length)
    for load in loads[1:]:
        load.wait()

    def near_head(h):
        q_heads[h] = wide_a[pl.ds(h, length, stride=heads), :].astype(jnp.bfloat16)
        level = levels[...]
        for ti in range(length // NEAR_TILE):
            cols = pl.ds(ti * NEAR_TILE, NEAR_TILE)
            query = q_heads[h, cols, :]
            pieces = []
            for si in range(ti + 1):
                scores = nt_dot(k_heads[h, pl.ds(si * NEAR_TILE, NEAR_TILE), :], query)
                if si < ti:
                    weighted = scores * w_in[h, pl.ds(log2(NEAR_TILE) + (ti ^ si).bit_length(), 1), cols]
                else:
                    columns = []
                    for a in range(NEAR_TILE // SUB):
                        at = pl.ds(ti * NEAR_TILE + a * SUB, SUB)
                        parts = []
                        for c in range(NEAR_TILE // SUB):
                            block = scores[c * SUB : (c + 1) * SUB, a * SUB : (a + 1) * SUB]
                            if c < a:
                                parts.append(block * w_in[h, pl.ds(log2(SUB) + (a ^ c).bit_length(), 1), at])
                            elif c > a:
                                parts.append(jnp.zeros_like(block))
                            else:
                                mixing = jnp.zeros((SUB, SUB), jnp.float32)
                                for n in range(log2(SUB) + 1):
                                    mixing = jnp.where(level == n, w_in[h, pl.ds(n, 1), at], mixing)
                                parts.append(mixing * block)
                        columns.append(jnp.concatenate(parts, 0))
                    weighted = jnp.concatenate(columns, 1)
                pieces.append(weighted.astype(jnp.bfloat16))
            near[h, :, cols] = jnp.dot(
                v_turned[h, :, pl.ds(0, (ti + 1) * NEAR_TILE)], jnp.concatenate(pieces, 0),
                preferred_element_type=jnp.float32,
            )

    def add_up(b, p):
        if b < bits - 1:
            where = rows_of(p)
            sums[b + 1, where, :] = sums[b, where, :] + buckets[b, where, :]

    def when_low(b, do):
        if b < bits - 1 and b != core:
            do()
        else:
            pl.when(bit[b] == 0)(do)

    def when_high(b, do):
        if b < bits - 1 and b != core:
            do()
        else:
            pl.when(bit[b] == 1)(do)

    def when_gateway(b, do, yes=1):
        pl.when(gateway(b) == yes)(do)

    def by_core(m, away=False):
        return 2 * m + (1 - bit[core] if away else bit[core])

    events = []
    free = {}

    def flight(link, ready, step, latency):
        end = max(free.get(link, 0), ready) + step
        free[link] = end
        return end + latency

    def event(at, do, *given):
        events.append((at, functools.partial(do, *given)))

    outer = (1 - gateway(top)) * bit[top]

    def held_back(b, side, i):
        return lean and b == 1 and side is other and i >= half // 2

    def begin(b, side, i):
        p = side(i)
        if b < 2:
            go = sends_1
            if held_back(b, side, i):
                go = go * (1 - bit[top] * gateway(top))
            when_lean(b, go, lambda: cross(b, p).start())
        elif b < core:
            if side is mine:
                when_gateway(b, lambda: cross(b, p).start())
        elif b == core:
            if side is mine:
                cross(b, p).start()
            else:
                when_low(b, lambda: cross(b, p).start())

    def arrived(b, side, i, kind=None):
        def do():
            p = side(i)
            cross(b, p).wait_recv()
            add_up(b, p)
            begin(b + 1, side, i)
        if kind is None:
            when_lean(b, takes_1, do)
        else:
            pl.when(takes_1 * (1 - outer if kind == 0 else outer) > 0)(do)

    def cross_arrived(b, i):
        def do():
            p = mine(i)
            cross(b, p).wait_recv()

            def on():
                relay(b, p).start()
                share(b, p).start()
                if b == top and held_back(1, other, i):
                    cross(1, other(i)).start()
            when_top(b, on)
            add_up(b, p)
            begin(b + 1, mine, i)
        when_gateway(b, do)

    def relay_arrived(b, i):
        def do():
            p = mine(i)
            relay(b, p).wait_recv()
            share(b, p).start()
            add_up(b, p)
            begin(b + 1, mine, i)
        when_gateway(b, lambda: when_top(b, do), 0)

    def share_arrived(b, yes, i):
        def do():
            p = other(i)
            share(b, p).wait_recv()
            add_up(b, p)
            begin(b + 1, other, i)
        when_gateway(b, lambda: when_top(b, do), yes)

    def when_outer(yes, do):
        pl.when(outer == yes)(do)

    def outer_pair(m):
        def do():
            for i in (2 * m, 2 * m + 1):
                cross(core, mine(i)).wait_recv()
            add_up(core, mine(by_core(m)))
            begin_far(core + 1, m)
        when_outer(1, do)

    def core_pair(m):
        def do():
            for i in (2 * m, 2 * m + 1):
                cross(core, mine(i)).wait_recv()
            add_up(core, mine(by_core(m)))

            @pl.when((1 - bit[top]) * bit[core] == 1)
            def _():
                for i in (2 * m, 2 * m + 1):
                    for n in range(1, len(targets)):
                        spread(mine(i), n, i).start()

            begin_far(core + 1, m)
        when_gateway(top, do)

    def low_arrived(side, yes, i):
        @pl.when((1 - bit[top]) * bit[core] == 1)
        def _():
            when_gateway(top, lambda: spread(side(i), 0, i).wait_recv(), yes)

    def core_arrived(side, yes, i):
        def do():
            when_high(core, lambda: cross(core, side(i)).wait_recv())
        when_gateway(top, lambda: when_top(top, do), yes)

    def passed_on(m):
        return m == half // 2 - 1

    def forward(b, p, n, m):
        where = rows_of(p)
        return pltpu.make_async_remote_copy(
            src_ref=buckets.at[b, where], dst_ref=buckets.at[b, where],
            send_sem=send_sem.at[(3 * b + 1) * heads + n * (half // 2) + m], recv_sem=recv_sem.at[3 * b * heads + p],
            device_id=peer(targets[n]), device_id_type=MESH_ID,
        )

    def each_aim(b, m, do):
        def one(n):
            do(far_copy(b, mine(by_core(m)), n, m))
        one(0)

        @pl.when(outer == 0)
        def _():
            for n in range(1, len(targets)):
                if n == 2:
                    if not passed_on(m):
                        pl.when(bit[top] == 0)(lambda: one(2))
                elif passed_on(m):
                    pl.when(bit[top] == 1)(lambda: one(n))
                else:
                    one(n)

    def each_forward(b, m, do):
        if passed_on(m):
            @pl.when((1 - bit[top]) * gateway(top) == 1)
            def _():
                for n in range(1, len(targets)):
                    do(forward(b, mine(by_core(m)), n, m))

    def landing(side, kind, m):
        if side is mine:
            if kind == 0:
                return gateway(top) == 1 if passed_on(m) else outer == 0
            return outer == 1 if kind == 1 else (1 - gateway(top)) * (1 - bit[top]) == 1
        if kind == 0:
            return bit[top] == 1 if passed_on(m) else bit[top] >= 0
        return bit[top] == 0

    def begin_far(b, m):
        if b < bits:
            when_low(b, lambda: each_aim(b, m, lambda c: c.start()))

    def far_arrived(b, side, kind, m):
        p = side(by_core(m))

        def take():
            far_copy(b, p, 0, 0).wait_recv()
            share(b, p).start()
            if side is mine and kind == 0:
                each_forward(b, m, lambda c: c.start())

        def do():
            when_high(b, take)
            if side is mine and kind < 2 and b < bits - 1:
                @pl.when(gateway(top) + kind > 0)
                def _():
                    add_up(b, p)
                    begin_far(b + 1, m)
        pl.when(landing(side, kind, m))(do)

    def far_share_arrived(b, side, kind, m):
        def do():
            when_high(b, lambda: share(b, side(by_core(m, True))).wait_recv())
        pl.when(landing(side, kind, m))(do)

    when = {}
    for n, (side, i) in enumerate([(mine, i) for i in range(half)] + [(other, i) for i in range(half)]):
        when[side, i] = flight(0, STATE_TIME * (n + 1), STEP, LATENCY)
    for b in range(2):
        later = {}
        for (side, i), at in sorted(when.items(), key=lambda e: e[1]):
            if held_back(b, side, i):
                event(at, arrived, b, side, i, 0)
            else:
                event(at, arrived, b, side, i)
            later[side, i] = flight(1, at, STEP, LATENCY)
        if b == 0:
            when = later
    whole_at = dict(when)
    early = {}
    for b in range(2, core):
        later = {}
        for i in range(half):
            at = flight(("gate", b), when[mine, i], STEP, LATENCY)
            event(at, cross_arrived, b, i)
            early[i] = at
            near_share = max(flight(("share", b), at, STEP, LATENCY), when[other, i] + 0.01)
            event(near_share, share_arrived, b, 1, i)
            relayed = max(flight(("relay", b), at, STEP, LATENCY), when[mine, i] + 0.01)
            event(relayed, relay_arrived, b, i)
            last = max(flight(("last", b), relayed, STEP, LATENCY), when[other, i] + 0.01)
            if b == top and held_back(1, other, i):
                event(relayed + STEP, arrived, 1, other, i, 1)
                whole_at[other, i] = max(whole_at[other, i], relayed + STEP)
                last = max(last, relayed + STEP + 0.02)
            event(last, share_arrived, b, 0, i)
            later[mine, i] = relayed
            later[other, i] = last
            if b == core - 1:
                event(near_share + CORE_LATENCY, core_arrived, other, 1, i)
                if i % 2 == 1:
                    event(relayed + CORE_LATENCY, outer_pair, i // 2)
                event(last + CORE_LATENCY, core_arrived, other, 0, i)
        when = later
    done = {i: max(when[mine, i], when[other, i]) + CORE_LATENCY for i in range(half)}
    for m in range(half // 2):
        at = early[2 * m + 1] + CORE_LATENCY
        event(at, core_pair, m)
        for i in (2 * m, 2 * m + 1):
            landed = flight("low", at, STEP, LATENCY + 0.5)
            event(landed, low_arrived, other, 1, i)
            event(landed, low_arrived, mine, 0, i)
            event(landed + 0.5, low_arrived, other, 0, i)
        outer_at = when[mine, 2 * m + 1] + CORE_LATENCY
        for b in range(core + 1, bits):
            for side in (mine, other):
                landed = flight(b, at, STEP, LATENCY + 0.7)
                event(landed, far_arrived, b, side, 0, m)
                event(landed + CORE_LATENCY, far_share_arrived, b, side, 0, m)
            passed = landed
            if passed_on(m):
                passed = flight(("forward", b), landed, STEP, LATENCY + 0.4)
                for side in (mine, other):
                    event(passed, far_arrived, b, side, 2, m)
                    event(passed + CORE_LATENCY, far_share_arrived, b, side, 2, m)
            outer_at = flight(("outer", b), outer_at, STEP, LATENCY)
            event(outer_at, far_arrived, b, mine, 1, m)
            event(outer_at + CORE_LATENCY, far_share_arrived, b, mine, 1, m)
            at = landed
            landed = max(landed, outer_at, passed)
            for i in (2 * m, 2 * m + 1):
                done[i] = max(done[i], landed + CORE_LATENCY)

    def far_head(h, chosen, last):
        where = pl.ds(pl.multiple_of(h * width, width), width)
        high = []
        low = []
        for b in chosen:
            whole = jnp.where(bit[b] == 1, buckets[b, where, :], 0.0)
            top = whole.astype(jnp.bfloat16)
            high.append(top)
            low.append((whole - top.astype(jnp.float32)).astype(jnp.bfloat16))
        both = jnp.concatenate([jnp.concatenate(high, 0), jnp.concatenate(low, 0)], 1)
        for ti in range(length // TILE):
            cols = pl.ds(ti * TILE, TILE)
            query = q_heads[h, cols, :]
            products = nt_dot(both, jnp.concatenate([query, query], 1))
            total = near[h, :, cols]
            for n, b in enumerate(chosen):
                total = total + products[n * width : (n + 1) * width] * w_in[h, pl.ds(local_bits + 1 + b, 1), cols]
            if last:
                scale = lax.rsqrt(jnp.mean(total * total, 0, keepdims=True) + EPSILON)
                wide_b[pl.ds(ti * TILE * heads + h, TILE, stride=heads), :] = (total * scale).T
            else:
                near[h, :, cols] = total

    first = [0, 1]
    last = list(range(2, bits))
    final = [max(done[2 * m], done[2 * m + 1]) for m in range(half // 2)]

    def sent_early(i, _):
        for side in (mine, other):
            p = side(i)
            cross(0, p).wait_send()
            when_lean(1, sends_1, lambda: cross(1, p).wait_send())
        for b in range(2, core):
            when_gateway(b, lambda: cross(b, mine(i)).wait_send())
        return 0

    loops = [
        (heads, NEAR_TIME, [0] * heads, lambda i: near_head(i)),
        (
            half // 2, 0.66, [whole_at[mine, 2 * i + 1] for i in range(half // 2)],
            lambda i: (far_head(mine(2 * i), first, False), far_head(mine(2 * i + 1), first, False)),
        ),
        (
            half // 2, 0.66, [whole_at[other, 2 * i + 1] for i in range(half // 2)],
            lambda i: (far_head(other(2 * i), first, False), far_head(other(2 * i + 1), first, False)),
        ),
        (half // 2, 1.3, final, lambda i: [far_head(side(2 * i + n), last, True) for side in (mine, other) for n in range(2)]),
    ]
    waiting = sorted(events, key=lambda e: e[0])
    clock = STATE_TIME * heads
    for count, cost, needs, work in loops:
        slots = []
        for need in needs:
            slots.append([])
            while waiting and waiting[0][0] <= max(clock, need + 0.02):
                at, do = waiting.pop(0)
                slots[-1].append(do)
                clock = max(clock, at)
            clock += cost

        def one(i, _, slots=slots, work=work):
            for at, group in enumerate(slots):
                def run(group=group):
                    for do in group:
                        do()
                if group:
                    pl.when(i == at)(run)
            work(i)
            return 0

        if needs is final:
            lax.fori_loop(0, half, sent_early, 0)
        lax.fori_loop(0, count, one, 0)
    assert not waiting

    def sent(i, _):
        for side in (mine, other):
            p = side(i)
            amount = (1 - bit[core]) * bit[top]
            if side is mine:
                amount = gateway(top) + bit[top]

            @pl.when(amount > 0)
            def _():
                cross(core, p).wait_send()
        for b in range(2, core):
            when_top(b, lambda: share(b, mine(i)).wait_send())

            def do():
                when_top(b, lambda: relay(b, mine(i)).wait_send())
            when_gateway(b, do)

        @pl.when((1 - bit[top]) * bit[core] * gateway(top) == 1)
        def _():
            for n in range(1, len(targets)):
                spread(mine(i), n, i).wait_send()
        return 0

    lax.fori_loop(0, half, sent, 0)

    def far_sent(m):
        for b in range(core + 1, bits):
            def done_far():
                when_low(b, lambda: each_aim(b, m, lambda c: c.wait_send()))
            pl.when(gateway(top) + bit[top] > 0)(done_far)

            def do_share():
                each_forward(b, m, lambda c: c.wait_send())
                for side in (mine, other):
                    share(b, side(by_core(m))).wait_send()
            when_high(b, do_share)

    for m in range(half // 2):
        far_sent(m)


def per_device(query, key, value, level_weight):
    length, heads, width = query.shape
    short_bits = log2(lax.axis_size("short"))
    long_bits = log2(lax.axis_size("long"))
    bits = short_bits + long_bits
    rows = heads * width
    copies = 3 * bits * heads + 2 * heads
    level_weight = jnp.transpose(level_weight, (1, 0, 2))
    total = pl.pallas_call(
        functools.partial(kernel, short_bits, long_bits, heads, length, width),
        out_shape=pltpu.VMEM((length * heads, width), jnp.float32),
        in_specs=[pl.BlockSpec(memory_space=pl.ANY)] * 4,
        out_specs=pl.BlockSpec(memory_space=pltpu.VMEM),
        scratch_shapes=[
            pltpu.VMEM(query.shape, jnp.bfloat16),
            pltpu.VMEM(query.shape, jnp.bfloat16),
            pltpu.VMEM(query.shape, jnp.bfloat16),
            pltpu.VMEM((heads, level_weight.shape[0], length), jnp.float32),
            pltpu.VMEM((length * heads, width), jnp.float32),
            pltpu.VMEM((heads, length, width), jnp.bfloat16),
            pltpu.VMEM((heads, length, width), jnp.bfloat16),
            pltpu.VMEM((heads, width, length), jnp.bfloat16),
            pltpu.VMEM((heads, width, length), jnp.float32),
            pltpu.VMEM((SUB, SUB), jnp.int32),
            pltpu.VMEM((bits, rows, width), jnp.float32),
            pltpu.VMEM((bits, rows, width), jnp.float32),
            pltpu.SemaphoreType.DMA((copies,)),
            pltpu.SemaphoreType.DMA((copies,)),
            pltpu.SemaphoreType.DMA((2 * CHUNKS + 1 + heads,)),
        ],
        compiler_params=pltpu.CompilerParams(
            collective_id=0, has_side_effects=True, vmem_limit_bytes=52 * 1024 * 1024
        ),
    )(query, key, value, level_weight)
    return total.reshape(query.shape).astype(jnp.bfloat16)


def solution(mesh):
    rows = P(("long", "short"), None)
    return jax.shard_map(
        per_device,
        mesh=mesh,
        in_specs=(rows, rows, rows, P(None, None, ("long", "short"))),
        out_specs=rows,
        check_vma=False,
    )
```

```python
import functools

import jax
import jax.numpy as jnp
from jax import lax
from jax.experimental import pallas as pl
from jax.experimental.pallas import tpu as pltpu
from jax.sharding import PartitionSpec as P

EPSILON = 1e-06
TILE = 256
NEAR_TILE = 512
SUB = 128
STATE_TIME = 0.43
NEAR_TIME = 0.95
STEP = 1.31
LATENCY = 2.2
CORE_LATENCY = 1.0
CHUNKS = 4
MESH_ID = pl.DeviceIdType.MESH


def log2(n):
    return n.bit_length() - 1


def subsets(bits):
    found = [tuple(b for i, b in enumerate(bits) if mask >> i & 1) for mask in range(1 << len(bits))]
    return sorted(found, key=len)


def nt_dot(a, b):
    return lax.dot_general(a, b, (((1,), (1,)), ((), ())), preferred_element_type=jnp.float32)


def kernel(
    short_bits, long_bits, heads, length, width,
    q_ref, k_ref, v_ref, w_ref, wide_b,
    k_in, v_in, q_in, w_in, wide_a, q_heads, k_heads, v_turned, near, levels, sums, buckets, send_sem, recv_sem, load_sem,
):
    bits = short_bits + long_bits
    rows = heads * width
    local_bits = log2(length)
    short_pos = lax.axis_index("short")
    long_pos = lax.axis_index("long")
    bit = [(short_pos // (1 << b)) % 2 for b in range(short_bits)]
    bit += [(long_pos // (1 << b)) % 2 for b in range(long_bits)]

    core = short_bits
    half = heads // 2
    targets = subsets([0, core - 2])

    def gateway(b):
        return bit[b - 1] + bit[b] - 2 * bit[b - 1] * bit[b]

    def peer(flips):
        short = short_pos
        long = long_pos
        for b in flips:
            if b < short_bits:
                short = short + (1 - 2 * bit[b]) * (1 << b)
            else:
                long = long + (1 - 2 * bit[b]) * (1 << b - short_bits)
        return {"short": short, "long": long}

    def mine(i):
        return bit[0] * half + i

    def other(i):
        return (1 - bit[0]) * half + i

    def rows_of(p):
        return pl.ds(pl.multiple_of(p * width, width), width)

    def copy(src, dst, b, p, bank, sent, to):
        where = rows_of(p)
        base = (3 * b + bank) * heads
        return pltpu.make_async_remote_copy(
            src_ref=src.at[b, where], dst_ref=dst.at[b, where],
            send_sem=send_sem.at[base + sent], recv_sem=recv_sem.at[base + p],
            device_id=peer(to), device_id_type=MESH_ID,
        )

    def cross(b, p):
        return copy(sums, buckets, b, p, 0, p, (b,) if b < 2 or b >= core else (b - 1, b))

    def relay(b, p):
        return copy(buckets, buckets, b, p, 1, p, (b - 1,))

    def share(b, p):
        return copy(buckets, buckets, b, p, 2, p, (0,) if b < core else (core,))

    top = core - 1
    lean = core - 2 == 1
    sends_1 = bit[top] + 1 - bit[1]
    takes_1 = bit[top] + bit[1]

    def spread(p, n, i):
        where = rows_of(p)
        base = 3 * bits * heads
        return pltpu.make_async_remote_copy(
            src_ref=buckets.at[core, where], dst_ref=buckets.at[core, where],
            send_sem=send_sem.at[base + n * half + i], recv_sem=recv_sem.at[base + p],
            device_id=peer(targets[n]), device_id_type=MESH_ID,
        )

    def when_lean(b, amount, do):
        if b == 1 and lean:
            pl.when(amount > 0)(do)
        else:
            do()

    def when_top(b, do):
        if b == top:
            pl.when(bit[top] == 1)(do)
        else:
            do()

    def far_copy(b, p, n, m):
        return copy(sums, buckets, b, p, 0, n * (half // 2) + m, (b,) + targets[n])

    peers = [(b,) for b in (0, 1)] + [(b,) for b in range(1, core - 1) if b > 1]
    peers += [(0, core - 2), (core,)] + [(b,) + c for b in range(core + 1, bits) for c in targets]

    chunk = length // CHUNKS
    first_loads = []
    for c in range(CHUNKS):
        for n, (src, dst) in enumerate([(k_ref, k_in), (v_ref, v_in)]):
            at = pl.ds(c * chunk, chunk)
            first_loads.append(pltpu.make_async_copy(src.at[at], dst.at[at], load_sem.at[2 * c + n]))
    loads = [pltpu.make_async_copy(q_ref, q_in, load_sem.at[2 * CHUNKS])]
    for h in range(heads):
        loads.append(pltpu.make_async_copy(w_ref.at[:, h, :], w_in.at[h], load_sem.at[2 * CHUNKS + 1 + h]))
    for load in first_loads:
        load.start()

    barrier = pltpu.get_barrier_semaphore()
    for flips in peers:
        pl.semaphore_signal(barrier, inc=1, device_id=peer(flips), device_id_type=MESH_ID)
    greeted = len(peers)
    for b in range(2, core):
        @pl.when(gateway(b) == 1)
        def _():
            pl.semaphore_signal(barrier, inc=1, device_id=peer((b - 1, b)), device_id_type=MESH_ID)
        greeted = greeted + gateway(b)

    part = 64

    def widen(src, dst, start, stop):
        def step(i, _):
            at = pl.multiple_of(i * part, part)
            x = src[pl.ds(at, part)].astype(jnp.float32)
            dst[pl.ds(pl.multiple_of(at * heads, part * heads), part * heads), :] = x.reshape(part * heads, width)
            return 0
        lax.fori_loop(start // part, stop // part, step, 0)

    for c in range(CHUNKS):
        for n, (src, dst) in enumerate([(k_in, wide_a), (v_in, wide_b)]):
            first_loads[2 * c + n].wait()
            if c == CHUNKS - 1 and n == 1:
                for load in loads:
                    load.start()
            widen(src, dst, c * chunk, (c + 1) * chunk)

    def state_of(i):
        h = (1 - bit[0] + i // half * (2 * bit[0] - 1)) * half + i % half
        key = wide_a[pl.ds(h, length, stride=heads), :].astype(jnp.bfloat16)
        turned = wide_b[pl.ds(h, length, stride=heads), :].T.astype(jnp.bfloat16)
        k_heads[h] = key
        v_turned[h] = turned
        sums[0, rows_of(h), :] = jnp.dot(turned, key, preferred_element_type=jnp.float32)
        return h

    def state_pair(n, _):
        first_two = [state_of(2 * n), state_of(2 * n + 1)]

        @pl.when(n == 0)
        def _():
            pl.semaphore_wait(barrier, greeted)

        for h in first_two:
            cross(0, h).start()
        return 0

    lax.fori_loop(0, half, state_pair, 0)

    row = lax.broadcasted_iota(jnp.int32, (SUB, SUB), 0)
    col = lax.broadcasted_iota(jnp.int32, (SUB, SUB), 1)
    differ = jnp.bitwise_xor(row, col)
    table = jnp.zeros((SUB, SUB), jnp.int32)
    for b in range(log2(SUB)):
        table = table + (differ >= 1 << b).astype(jnp.int32)
    levels[...] = jnp.where(row <= col, table, -1)

    loads[0].wait()
    widen(q_in, wide_a, 0, length)
    for load in loads[1:]:
        load.wait()

    def near_head(h):
        q_heads[h] = wide_a[pl.ds(h, length, stride=heads), :].astype(jnp.bfloat16)
        level = levels[...]
        for ti in range(length // NEAR_TILE):
            cols = pl.ds(ti * NEAR_TILE, NEAR_TILE)
            query = q_heads[h, cols, :]
            pieces = []
            for si in range(ti + 1):
                scores = nt_dot(k_heads[h, pl.ds(si * NEAR_TILE, NEAR_TILE), :], query)
                if si < ti:
                    weighted = scores * w_in[h, pl.ds(log2(NEAR_TILE) + (ti ^ si).bit_length(), 1), cols]
                else:
                    columns = []
                    for a in range(NEAR_TILE // SUB):
                        at = pl.ds(ti * NEAR_TILE + a * SUB, SUB)
                        parts = []
                        for c in range(NEAR_TILE // SUB):
                            block = scores[c * SUB : (c + 1) * SUB, a * SUB : (a + 1) * SUB]
                            if c < a:
                                parts.append(block * w_in[h, pl.ds(log2(SUB) + (a ^ c).bit_length(), 1), at])
                            elif c > a:
                                parts.append(jnp.zeros_like(block))
                            else:
                                mixing = jnp.zeros((SUB, SUB), jnp.float32)
                                for n in range(log2(SUB) + 1):
                                    mixing = jnp.where(level == n, w_in[h, pl.ds(n, 1), at], mixing)
                                parts.append(mixing * block)
                        columns.append(jnp.concatenate(parts, 0))
                    weighted = jnp.concatenate(columns, 1)
                pieces.append(weighted.astype(jnp.bfloat16))
            near[h, :, cols] = jnp.dot(
                v_turned[h, :, pl.ds(0, (ti + 1) * NEAR_TILE)], jnp.concatenate(pieces, 0),
                preferred_element_type=jnp.float32,
            )

    def add_up(b, p):
        if b < bits - 1:
            where = rows_of(p)
            sums[b + 1, where, :] = sums[b, where, :] + buckets[b, where, :]

    def when_low(b, do):
        if b < bits - 1 and b != core:
            do()
        else:
            pl.when(bit[b] == 0)(do)

    def when_high(b, do):
        if b < bits - 1 and b != core:
            do()
        else:
            pl.when(bit[b] == 1)(do)

    def when_gateway(b, do, yes=1):
        pl.when(gateway(b) == yes)(do)

    def by_core(m, away=False):
        return 2 * m + (1 - bit[core] if away else bit[core])

    events = []
    free = {}

    def flight(link, ready, step, latency):
        end = max(free.get(link, 0), ready) + step
        free[link] = end
        return end + latency

    def event(at, do, *given):
        events.append((at, functools.partial(do, *given)))

    outer = (1 - gateway(top)) * bit[top]

    def held_back(b, side, i):
        return lean and b == 1 and side is other and i >= half // 2

    def begin(b, side, i):
        p = side(i)
        if b < 2:
            go = sends_1
            if held_back(b, side, i):
                go = go * (1 - bit[top] * gateway(top))
            when_lean(b, go, lambda: cross(b, p).start())
        elif b < core:
            if side is mine:
                when_gateway(b, lambda: cross(b, p).start())
        elif b == core:
            if side is mine:
                cross(b, p).start()
            else:
                when_low(b, lambda: cross(b, p).start())

    def arrived(b, side, i, kind=None):
        def do():
            p = side(i)
            cross(b, p).wait_recv()
            add_up(b, p)
            begin(b + 1, side, i)
        if kind is None:
            when_lean(b, takes_1, do)
        else:
            pl.when(takes_1 * (1 - outer if kind == 0 else outer) > 0)(do)

    def cross_arrived(b, i):
        def do():
            p = mine(i)
            cross(b, p).wait_recv()

            def on():
                relay(b, p).start()
                share(b, p).start()
                if b == top and held_back(1, other, i):
                    cross(1, other(i)).start()
            when_top(b, on)
            add_up(b, p)
            begin(b + 1, mine, i)
        when_gateway(b, do)

    def relay_arrived(b, i):
        def do():
            p = mine(i)
            relay(b, p).wait_recv()
            share(b, p).start()
            add_up(b, p)
            begin(b + 1, mine, i)
        when_gateway(b, lambda: when_top(b, do), 0)

    def share_arrived(b, yes, i):
        def do():
            p = other(i)
            share(b, p).wait_recv()
            add_up(b, p)
            begin(b + 1, other, i)
        when_gateway(b, lambda: when_top(b, do), yes)

    def when_outer(yes, do):
        pl.when(outer == yes)(do)

    def outer_pair(m):
        def do():
            for i in (2 * m, 2 * m + 1):
                cross(core, mine(i)).wait_recv()
            add_up(core, mine(by_core(m)))
            begin_far(core + 1, m)
        when_outer(1, do)

    def core_pair(m):
        def do():
            for i in (2 * m, 2 * m + 1):
                cross(core, mine(i)).wait_recv()
            add_up(core, mine(by_core(m)))

            @pl.when((1 - bit[top]) * bit[core] == 1)
            def _():
                for i in (2 * m, 2 * m + 1):
                    for n in range(1, len(targets)):
                        spread(mine(i), n, i).start()

            begin_far(core + 1, m)
        when_gateway(top, do)

    def low_arrived(side, yes, i):
        @pl.when((1 - bit[top]) * bit[core] == 1)
        def _():
            when_gateway(top, lambda: spread(side(i), 0, i).wait_recv(), yes)

    def core_arrived(side, yes, i):
        def do():
            when_high(core, lambda: cross(core, side(i)).wait_recv())
        when_gateway(top, lambda: when_top(top, do), yes)

    def passed_on(m):
        return m == half // 2 - 1

    def forward(b, p, n, m):
        where = rows_of(p)
        return pltpu.make_async_remote_copy(
            src_ref=buckets.at[b, where], dst_ref=buckets.at[b, where],
            send_sem=send_sem.at[(3 * b + 1) * heads + n * (half // 2) + m], recv_sem=recv_sem.at[3 * b * heads + p],
            device_id=peer(targets[n]), device_id_type=MESH_ID,
        )

    def each_aim(b, m, do):
        def one(n):
            do(far_copy(b, mine(by_core(m)), n, m))
        one(0)

        @pl.when(outer == 0)
        def _():
            for n in range(1, len(targets)):
                if n == 2:
                    if not passed_on(m):
                        pl.when(bit[top] == 0)(lambda: one(2))
                elif passed_on(m):
                    pl.when(bit[top] == 1)(lambda: one(n))
                else:
                    one(n)

    def each_forward(b, m, do):
        if passed_on(m):
            @pl.when((1 - bit[top]) * gateway(top) == 1)
            def _():
                for n in range(1, len(targets)):
                    do(forward(b, mine(by_core(m)), n, m))

    def landing(side, kind, m):
        if side is mine:
            if kind == 0:
                return gateway(top) == 1 if passed_on(m) else outer == 0
            return outer == 1 if kind == 1 else (1 - gateway(top)) * (1 - bit[top]) == 1
        if kind == 0:
            return bit[top] == 1 if passed_on(m) else bit[top] >= 0
        return bit[top] == 0

    def begin_far(b, m):
        if b < bits:
            when_low(b, lambda: each_aim(b, m, lambda c: c.start()))

    def far_arrived(b, side, kind, m):
        p = side(by_core(m))

        def take():
            far_copy(b, p, 0, 0).wait_recv()
            share(b, p).start()
            if side is mine and kind == 0:
                each_forward(b, m, lambda c: c.start())

        def do():
            when_high(b, take)
            if side is mine and kind < 2 and b < bits - 1:
                @pl.when(gateway(top) + kind > 0)
                def _():
                    add_up(b, p)
                    begin_far(b + 1, m)
        pl.when(landing(side, kind, m))(do)

    def far_share_arrived(b, side, kind, m):
        def do():
            when_high(b, lambda: share(b, side(by_core(m, True))).wait_recv())
        pl.when(landing(side, kind, m))(do)

    when = {}
    for n, (side, i) in enumerate([(mine, i) for i in range(half)] + [(other, i) for i in range(half)]):
        when[side, i] = flight(0, STATE_TIME * (n + 1), STEP, LATENCY)
    for b in range(2):
        later = {}
        for (side, i), at in sorted(when.items(), key=lambda e: e[1]):
            if held_back(b, side, i):
                event(at, arrived, b, side, i, 0)
            else:
                event(at, arrived, b, side, i)
            later[side, i] = flight(1, at, STEP, LATENCY)
        if b == 0:
            when = later
    whole_at = dict(when)
    early = {}
    for b in range(2, core):
        later = {}
        for i in range(half):
            at = flight(("gate", b), when[mine, i], STEP, LATENCY)
            event(at, cross_arrived, b, i)
            early[i] = at
            near_share = max(flight(("share", b), at, STEP, LATENCY), when[other, i] + 0.01)
            event(near_share, share_arrived, b, 1, i)
            relayed = max(flight(("relay", b), at, STEP, LATENCY), when[mine, i] + 0.01)
            event(relayed, relay_arrived, b, i)
            last = max(flight(("last", b), relayed, STEP, LATENCY), when[other, i] + 0.01)
            if b == top and held_back(1, other, i):
                event(relayed + STEP, arrived, 1, other, i, 1)
                whole_at[other, i] = max(whole_at[other, i], relayed + STEP)
                last = max(last, relayed + STEP + 0.02)
            event(last, share_arrived, b, 0, i)
            later[mine, i] = relayed
            later[other, i] = last
            if b == core - 1:
                event(near_share + CORE_LATENCY, core_arrived, other, 1, i)
                if i % 2 == 1:
                    event(relayed + CORE_LATENCY, outer_pair, i // 2)
                event(last + CORE_LATENCY, core_arrived, other, 0, i)
        when = later
    done = {i: max(when[mine, i], when[other, i]) + CORE_LATENCY for i in range(half)}
    for m in range(half // 2):
        at = early[2 * m + 1] + CORE_LATENCY
        event(at, core_pair, m)
        for i in (2 * m, 2 * m + 1):
            landed = flight("low", at, STEP, LATENCY + 0.5)
            event(landed, low_arrived, other, 1, i)
            event(landed, low_arrived, mine, 0, i)
            event(landed + 0.5, low_arrived, other, 0, i)
        outer_at = when[mine, 2 * m + 1] + CORE_LATENCY
        for b in range(core + 1, bits):
            for side in (mine, other):
                landed = flight(b, at, STEP, LATENCY + 0.7)
                event(landed, far_arrived, b, side, 0, m)
                event(landed + CORE_LATENCY, far_share_arrived, b, side, 0, m)
            passed = landed
            if passed_on(m):
                passed = flight(("forward", b), landed, STEP, LATENCY + 0.4)
                for side in (mine, other):
                    event(passed, far_arrived, b, side, 2, m)
                    event(passed + CORE_LATENCY, far_share_arrived, b, side, 2, m)
            outer_at = flight(("outer", b), outer_at, STEP, LATENCY)
            event(outer_at, far_arrived, b, mine, 1, m)
            event(outer_at + CORE_LATENCY, far_share_arrived, b, mine, 1, m)
            at = landed
            landed = max(landed, outer_at, passed)
            for i in (2 * m, 2 * m + 1):
                done[i] = max(done[i], landed + CORE_LATENCY)

    def far_head(h, chosen, last):
        where = pl.ds(pl.multiple_of(h * width, width), width)
        high = []
        low = []
        for b in chosen:
            whole = jnp.where(bit[b] == 1, buckets[b, where, :], 0.0)
            top = whole.astype(jnp.bfloat16)
            high.append(top)
            low.append((whole - top.astype(jnp.float32)).astype(jnp.bfloat16))
        both = jnp.concatenate([jnp.concatenate(high, 0), jnp.concatenate(low, 0)], 1)
        for ti in range(length // TILE):
            cols = pl.ds(ti * TILE, TILE)
            query = q_heads[h, cols, :]
            products = nt_dot(both, jnp.concatenate([query, query], 1))
            total = near[h, :, cols]
            for n, b in enumerate(chosen):
                total = total + products[n * width : (n + 1) * width] * w_in[h, pl.ds(local_bits + 1 + b, 1), cols]
            if last:
                scale = lax.rsqrt(jnp.mean(total * total, 0, keepdims=True) + EPSILON)
                wide_b[pl.ds(ti * TILE * heads + h, TILE, stride=heads), :] = (total * scale).T
            else:
                near[h, :, cols] = total

    first = [0, 1]
    last = list(range(2, bits))
    final = [max(done[2 * m], done[2 * m + 1]) for m in range(half // 2)]

    def sent_early(i, _):
        for side in (mine, other):
            p = side(i)
            cross(0, p).wait_send()
            when_lean(1, sends_1, lambda: cross(1, p).wait_send())
        for b in range(2, core):
            when_gateway(b, lambda: cross(b, mine(i)).wait_send())
        return 0

    loops = [
        (heads, NEAR_TIME, [0] * heads, lambda i: near_head(i)),
        (
            half // 2, 0.66, [whole_at[mine, 2 * i + 1] for i in range(half // 2)],
            lambda i: (far_head(mine(2 * i), first, False), far_head(mine(2 * i + 1), first, False)),
        ),
        (
            half // 2, 0.66, [whole_at[other, 2 * i + 1] for i in range(half // 2)],
            lambda i: (far_head(other(2 * i), first, False), far_head(other(2 * i + 1), first, False)),
        ),
        (half // 2, 1.3, final, lambda i: [far_head(side(2 * i + n), last, True) for side in (mine, other) for n in range(2)]),
    ]
    waiting = sorted(events, key=lambda e: e[0])
    clock = STATE_TIME * heads
    for count, cost, needs, work in loops:
        slots = []
        for need in needs:
            slots.append([])
            while waiting and waiting[0][0] <= max(clock, need + 0.02):
                at, do = waiting.pop(0)
                slots[-1].append(do)
                clock = max(clock, at)
            clock += cost

        def one(i, _, slots=slots, work=work):
            for at, group in enumerate(slots):
                def run(group=group):
                    for do in group:
                        do()
                if group:
                    pl.when(i == at)(run)
            work(i)
            return 0

        if needs is final:
            lax.fori_loop(0, half, sent_early, 0)
        lax.fori_loop(0, count, one, 0)
    assert not waiting

    def sent(i, _):
        for side in (mine, other):
            p = side(i)
            amount = (1 - bit[core]) * bit[top]
            if side is mine:
                amount = gateway(top) + bit[top]

            @pl.when(amount > 0)
            def _():
                cross(core, p).wait_send()
        for b in range(2, core):
            when_top(b, lambda: share(b, mine(i)).wait_send())

            def do():
                when_top(b, lambda: relay(b, mine(i)).wait_send())
            when_gateway(b, do)

        @pl.when((1 - bit[top]) * bit[core] * gateway(top) == 1)
        def _():
            for n in range(1, len(targets)):
                spread(mine(i), n, i).wait_send()
        return 0

    lax.fori_loop(0, half, sent, 0)

    def far_sent(m):
        for b in range(core + 1, bits):
            def done_far():
                when_low(b, lambda: each_aim(b, m, lambda c: c.wait_send()))
            pl.when(gateway(top) + bit[top] > 0)(done_far)

            def do_share():
                each_forward(b, m, lambda c: c.wait_send())
                for side in (mine, other):
                    share(b, side(by_core(m))).wait_send()
            when_high(b, do_share)

    for m in range(half // 2):
        far_sent(m)


def per_device(query, key, value, level_weight):
    length, heads, width = query.shape
    short_bits = log2(lax.axis_size("short"))
    long_bits = log2(lax.axis_size("long"))
    bits = short_bits + long_bits
    rows = heads * width
    copies = 3 * bits * heads + 2 * heads
    level_weight = jnp.transpose(level_weight, (1, 0, 2))
    total = pl.pallas_call(
        functools.partial(kernel, short_bits, long_bits, heads, length, width),
        out_shape=pltpu.VMEM((length * heads, width), jnp.float32),
        in_specs=[pl.BlockSpec(memory_space=pl.ANY)] * 4,
        out_specs=pl.BlockSpec(memory_space=pltpu.VMEM),
        scratch_shapes=[
            pltpu.VMEM(query.shape, jnp.bfloat16),
            pltpu.VMEM(query.shape, jnp.bfloat16),
            pltpu.VMEM(query.shape, jnp.bfloat16),
            pltpu.VMEM((heads, level_weight.shape[0], length), jnp.float32),
            pltpu.VMEM((length * heads, width), jnp.float32),
            pltpu.VMEM((heads, length, width), jnp.bfloat16),
            pltpu.VMEM((heads, length, width), jnp.bfloat16),
            pltpu.VMEM((heads, width, length), jnp.bfloat16),
            pltpu.VMEM((heads, width, length), jnp.float32),
            pltpu.VMEM((SUB, SUB), jnp.int32),
            pltpu.VMEM((bits, rows, width), jnp.float32),
            pltpu.VMEM((bits, rows, width), jnp.float32),
            pltpu.SemaphoreType.DMA((copies,)),
            pltpu.SemaphoreType.DMA((copies,)),
            pltpu.SemaphoreType.DMA((2 * CHUNKS + 1 + heads,)),
        ],
        compiler_params=pltpu.CompilerParams(
            collective_id=0, has_side_effects=True, vmem_limit_bytes=52 * 1024 * 1024
        ),
    )(query, key, value, level_weight)
    return total.reshape(query.shape).astype(jnp.bfloat16)


def solution(mesh):
    rows = P(("long", "short"), None)
    return jax.shard_map(
        per_device,
        mesh=mesh,
        in_specs=(rows, rows, rows, P(None, None, ("long", "short"))),
        out_specs=rows,
        check_vma=False,
    )
```
